32 devices in a mesh: grp: 2 (over x), span: 16 (over z, y, core).
Axes of the slice: x: 2, y: 2, z: 4, core: 2. Of those that a mesh axis runs over, the one named last changes fastest.
Arguments:
- first_exposure: bfloat16 [1920, 96, 192], P(('grp', 'span')), parts along dimension 0, may hold values from 0 to 30
- second_exposure: bfloat16 [1920, 96, 192], P(('grp', 'span')), parts along dimension 0, may hold values from 0 to 30
- windows: int32 [256], P(('grp', 'span')), parts along dimension 0, may hold values from 0 to 10239, as said below
- shifts: int32 [3, 256], P(None, ('grp', 'span')), parts along dimension 1, may hold values from -8 to 8, as said below
Outputs:
- smoothed_update: float32 [3, 160, 128], P(None, ('grp', 'span')), parts along dimension 1
The draws below stay inside these ranges and needn't reach their ends.
There are 2 independent parts, one for each index of `grp`. The reference program is written for one: setup_inputs(seed, part) draws one part's arguments, and reference() takes and returns one part's arrays. A program takes and returns all parts, laid end to end along the dimension named above; each array names one. Nothing has to cross between parts.
Inputs may be any that keep to these rules, and one draw needn't show every extreme that they name: The windows of one device are distinct nodes whose spanwise grid row j has j // 5 equal to that device's index along span; exactly 4 of them have j % 5 < 2. `shifts`: row 0 is the spanwise shift (at most 3 in size), row 1 the wall-normal one (at most 4 in size), row 2 the streamwise one (at most 8 in size).
All inputs are finite; a program needn't handle non-finite values.
Results may differ from the reference program's by a relative error of at most 0.0022.
Values may be sent and summed in bfloat16 or wider, within the bound.
A program may use at most 128 MiB of HBM per device.

```python
import jax
import jax.numpy as jnp
from jax import lax

W = 48
STRIDE = 12
CY = 60
NZ = 96
NX = 192
WIN_DEV = 8
DYM = 3
DZM = 4
DXM = 8
CAP = 4
NY = 960
GY = 80
GZ = 8
GX = 16
GZX = 128
WINDOWS = 128


def field_plan(key):
    base = jax.random.fold_in(key, 6173)
    keys = jax.random.split(base, 4)
    span_base = jax.random.randint(keys[0], (GY, 1, 1), -DYM, DYM + 1, dtype=jnp.int32)
    deep_base = jax.random.randint(keys[1], (GY, 1, 1), -DZM, DZM + 1, dtype=jnp.int32)
    along_base = jax.random.randint(keys[2], (GY, GZ, 1), -DXM, DXM + 1, dtype=jnp.int32)
    jitter = jax.random.randint(keys[3], (3, GY, GZ, GX), -1, 2, dtype=jnp.int32)
    shift_y = jnp.clip(span_base + jitter[0], -DYM, DYM)
    shift_z = jnp.clip(deep_base + jitter[1], -DZM, DZM)
    shift_x = jnp.clip(along_base + jitter[2], -DXM, DXM)
    return jnp.stack([shift_y, shift_z, shift_x]).astype(jnp.int32)


def window_plan(key):
    base = jax.random.fold_in(key, 4051)
    devices = WINDOWS // WIN_DEV
    tile_rows = CY // STRIDE
    lower_count = 2 * GZX
    upper_count = 3 * GZX
    keys = jax.random.split(base, 3)
    lower_scores = jax.random.randint(keys[0], (devices, lower_count), 0, 4096, dtype=jnp.int32) * lower_count
    lower_scores = lower_scores + jnp.arange(lower_count, dtype=jnp.int32)[None, :]
    lower_pick = jnp.argsort(lower_scores, axis=1)[:, :CAP].astype(jnp.int32)
    upper_scores = jax.random.randint(keys[1], (devices, upper_count), 0, 4096, dtype=jnp.int32) * upper_count
    upper_scores = upper_scores + jnp.arange(upper_count, dtype=jnp.int32)[None, :]
    upper_pick = jnp.argsort(upper_scores, axis=1)[:, :WIN_DEV - CAP].astype(jnp.int32) + lower_count
    chosen = jnp.concatenate([lower_pick, upper_pick], axis=1)
    order_scores = jax.random.randint(keys[2], (devices, WIN_DEV), 0, 4096, dtype=jnp.int32) * WIN_DEV
    order_scores = order_scores + jnp.arange(WIN_DEV, dtype=jnp.int32)[None, :]
    order = jnp.argsort(order_scores, axis=1).astype(jnp.int32)
    chosen = jnp.take_along_axis(chosen, order, axis=1)
    device_ids = jnp.arange(devices, dtype=jnp.int32)[:, None]
    nodes = (device_ids * tile_rows * GZX + chosen).reshape(-1)
    field = field_plan(key).reshape(3, -1)
    return (nodes, field[:, nodes])


def draw_windows(key, part):
    return window_plan(key)[0]


def draw_shifts(key, part):
    return window_plan(key)[1]


def lattice(key):
    margin_y = DYM + 1
    margin_z = DZM + 1
    margin_x = DXM + 1
    base = jax.random.fold_in(key, 7919)
    coarse = (GY + 6, GZ + 6, GX + 6)
    level = jax.random.uniform(base, coarse, jnp.float32, 0.0, jnp.log(10.0))
    cells = jnp.exp(level)
    cells = jnp.repeat(jnp.repeat(jnp.repeat(cells, STRIDE, 0), STRIDE, 1), STRIDE, 2)
    cells = cells[3 * STRIDE - margin_y:3 * STRIDE + NY + margin_y, 3 * STRIDE - margin_z:3 * STRIDE + NZ + margin_z, 3 * STRIDE - margin_x:3 * STRIDE + NX + margin_x]
    noise = jax.random.uniform(jax.random.fold_in(key, 1), cells.shape, jnp.float32)
    return (cells * noise, cells)


def draw_first_exposure(key, part):
    margin_y = DYM + 1
    margin_z = DZM + 1
    margin_x = DXM + 1
    field, cells = lattice(key)
    return field[margin_y:margin_y + NY, margin_z:margin_z + NZ, margin_x:margin_x + NX].astype(jnp.bfloat16)


def draw_second_exposure(key, part):
    margin_y = DYM + 1
    margin_z = DZM + 1
    margin_x = DXM + 1
    field, cells = lattice(key)
    whole_shift = field_plan(key)
    residual = jax.random.uniform(jax.random.fold_in(key, 5), (3, GY, GZ, GX), jnp.float32)
    slab_shape = (STRIDE + 2 * margin_y, NZ + 2 * margin_z, NX + 2 * margin_x)

    def one_row(row):
        slab = lax.dynamic_slice(field, (row * STRIDE, 0, 0), slab_shape)
        row_shift = jnp.repeat(jnp.repeat(whole_shift[:, row], STRIDE, 1), STRIDE, 2)
        row_rest = jnp.repeat(jnp.repeat(residual[:, row], STRIDE, 1), STRIDE, 2)
        span_idx = jnp.arange(STRIDE, dtype=jnp.int32)[:, None, None] + margin_y - row_shift[0][None]
        deep_idx = jnp.arange(NZ, dtype=jnp.int32)[None, :, None] + margin_z - row_shift[1][None]
        along_idx = jnp.arange(NX, dtype=jnp.int32)[None, None, :] + margin_x - row_shift[2][None]
        span_idx = jnp.broadcast_to(span_idx, (STRIDE, NZ, NX))
        deep_idx = jnp.broadcast_to(deep_idx, (STRIDE, NZ, NX))
        along_idx = jnp.broadcast_to(along_idx, (STRIDE, NZ, NX))
        rest_y = row_rest[0][None]
        rest_z = row_rest[1][None]
        rest_x = row_rest[2][None]
        total = jnp.zeros((STRIDE, NZ, NX), jnp.float32)
        for corner_y in range(2):
            weight_y = rest_y if corner_y == 0 else 1.0 - rest_y
            for corner_z in range(2):
                weight_z = rest_z if corner_z == 0 else 1.0 - rest_z
                for corner_x in range(2):
                    weight_x = rest_x if corner_x == 0 else 1.0 - rest_x
                    picked = slab[span_idx - 1 + corner_y, deep_idx - 1 + corner_z, along_idx - 1 + corner_x]
                    total = total + weight_y * weight_z * weight_x * picked
        return total
    rows = lax.map(one_row, jnp.arange(GY, dtype=jnp.int32)).reshape(NY, NZ, NX)
    inner_cells = cells[margin_y:margin_y + NY, margin_z:margin_z + NZ, margin_x:margin_x + NX]
    fresh = jax.random.uniform(jax.random.fold_in(key, 3), (NY, NZ, NX), jnp.float32)
    return (0.9 * rows + 0.1 * inner_cells * fresh).astype(jnp.bfloat16)


def setup_inputs(seed: int = 0, part: int = 0) -> dict:
    key_of = jax.random.split(jax.random.key(seed), 5)
    own_keys = jax.random.split(jax.random.fold_in(key_of[4], part), 5)
    first_exposure = draw_first_exposure(jax.random.fold_in(jax.random.fold_in(key_of[4], part), 71), part)
    second_exposure = draw_second_exposure(jax.random.fold_in(jax.random.fold_in(key_of[4], part), 71), part)
    windows = draw_windows(jax.random.fold_in(jax.random.fold_in(key_of[4], part), 71), part)
    shifts = draw_shifts(jax.random.fold_in(jax.random.fold_in(key_of[4], part), 71), part)
    return {"first_exposure": first_exposure, "second_exposure": second_exposure, "windows": windows, "shifts": shifts}


SHARP = 80.0
EPSILON = 1e-06

def window_terms(first_pad, second_pad, node, shift):
    half_width = W // 2
    node_row = node // GZX
    node_rest = node % GZX
    node_deep = node_rest // GX
    node_along = node_rest % GX
    centre_y = STRIDE * node_row + STRIDE // 2
    centre_z = STRIDE * node_deep + STRIDE // 2
    centre_x = STRIDE * node_along + STRIDE // 2
    first_window = lax.dynamic_slice(first_pad, (centre_y, centre_z, centre_x), (W, W, W))
    pad_y = 3 * CY
    pad_z = half_width + 1 + DZM
    pad_x = half_width + 1 + DXM
    start_y = (centre_y + shift[0] - half_width - 1 + pad_y).astype(jnp.int32)
    start_z = (centre_z + shift[1] - half_width - 1 + pad_z).astype(jnp.int32)
    start_x = (centre_x + shift[2] - half_width - 1 + pad_x).astype(jnp.int32)
    second_block = lax.dynamic_slice(second_pad, (start_y, start_z, start_x), (W + 2, W + 2, W + 2))
    first_wide = first_window.astype(jnp.float32)
    first_centred = (first_wide - jnp.mean(first_wide)).astype(jnp.bfloat16)
    second_wide = second_block.astype(jnp.float32)
    second_centred = (second_wide - jnp.mean(second_wide)).astype(jnp.bfloat16)
    first_back = first_centred.astype(jnp.float32)
    second_back = second_centred.astype(jnp.float32)
    energy_first = jnp.mean(first_back * first_back)
    energy_second = jnp.mean(second_back * second_back)
    normaliser = float(W) ** 3 * jnp.sqrt((energy_first + EPSILON) * (energy_second + EPSILON))
    collected = []
    for lag_y in range(3):
        for lag_z in range(3):
            for lag_x in range(3):
                shifted_piece = lax.slice(second_back, (lag_y, lag_z, lag_x), (lag_y + W, lag_z + W, lag_x + W))
                collected.append(jnp.sum(first_back * shifted_piece))
    coherence = jnp.stack(collected).reshape(3, 3, 3) / normaliser
    weights = jnp.exp(SHARP * coherence)
    weight_sum = jnp.sum(weights)
    lag_values = jnp.array([-1.0, 0.0, 1.0], jnp.float32)
    along_y = jnp.sum(weights * lag_values[:, None, None]) / weight_sum
    along_z = jnp.sum(weights * lag_values[None, :, None]) / weight_sum
    along_x = jnp.sum(weights * lag_values[None, None, :]) / weight_sum
    return jnp.stack([along_y, along_z, along_x])

def reference(first_exposure, second_exposure, windows, shifts):
    half_width = W // 2
    first_pad = jnp.pad(first_exposure, half_width)
    pad_z = half_width + 1 + DZM
    pad_x = half_width + 1 + DXM
    second_pad = jnp.pad(second_exposure, ((3 * CY, 3 * CY), (pad_z, pad_z), (pad_x, pad_x)))

    def one_window(window_item):
        return window_terms(first_pad, second_pad, window_item[0], window_item[1])
    corrections = lax.map(one_window, (windows, shifts.T))
    update = jnp.zeros((3, GY * GZX), jnp.float32).at[:, windows].set(corrections.T)
    field_grid = update.reshape(3, GY, GZ, GX)
    padded = jnp.pad(field_grid, ((0, 0), (1, 1), (1, 1), (1, 1)))
    neighbours = padded[:, 2:, 1:-1, 1:-1] + padded[:, :-2, 1:-1, 1:-1]
    neighbours = neighbours + padded[:, 1:-1, 2:, 1:-1] + padded[:, 1:-1, :-2, 1:-1]
    neighbours = neighbours + padded[:, 1:-1, 1:-1, 2:] + padded[:, 1:-1, 1:-1, :-2]
    smoothed = 0.4 * field_grid + 0.1 * neighbours
    return smoothed.reshape(3, GY, GZX)
```

```python
import functools

import jax
import jax.numpy as jnp
from jax import lax
from jax.experimental import pallas as pl
from jax.experimental.pallas import tpu as pltpu
from jax.sharding import PartitionSpec as P

W = 48
STRIDE = 12
DYM = 3
GZ = 8
GX = 16
GZX = 128
HALO = DYM + 1
HALF = W // 2
BW = W + 2
ROWS_TILE = 5
CY = STRIDE * ROWS_TILE
SPILL = 18
LOWER = 42
SLOTS = 4
TASKS = 16

SHARP = 80.0
EPSILON = 1e-06

F32 = jnp.float32
BF16 = jnp.bfloat16

PAD_X = 32
XR = 64
LANES = 128
SUB = 16
A_OFF = SPILL
A_PLANES = SPILL + CY + SPILL
B_OFF = SPILL + HALO
B_PLANES = B_OFF + CY + B_OFF
CHUNK = 10
PREP = 10


def sizes(n):
    total = n + 2
    out = []
    while total > 0:
        out.append(min(CHUNK, total))
        total -= CHUNK
    return out


def kernel(
    n, win, sh, win_hbm, sh_hbm, a_hbm, b_hbm, out,
    a_raw, b_raw, low_raw, high_raw, win_low, win_high, sh_low, sh_high,
    a_t, b_t, a_s, pivots, lines, stats, mine, low, high, send, recv, sems,
):
    nz, nx = a_hbm.shape[1], a_hbm.shape[2]
    x_blocks = a_t.shape[1]
    device = lax.axis_index("span")
    last = n - 1
    has_low, has_high = device > 0, device < last
    no_low, no_high = device == 0, device == last
    parts = CY // PREP
    loads = []
    for c in range(parts):
        rows = pl.ds(c * PREP, PREP)
        loads.append(pltpu.make_async_copy(b_hbm.at[rows], b_raw.at[rows], sems.at[2 * c]))
        loads.append(pltpu.make_async_copy(a_hbm.at[rows], a_raw.at[rows], sems.at[2 * c + 1]))
    for load in loads:
        load.start()

    barrier = pltpu.get_barrier_semaphore()

    def greet(to):
        pl.semaphore_signal(
            barrier, inc=1, device_id={"span": to}, device_id_type=pl.DeviceIdType.MESH
        )

    @pl.when(has_low)
    def _():
        greet(device - 1)

    @pl.when(has_high)
    def _():
        greet(device + 1)

    pl.semaphore_wait(barrier, has_low.astype(jnp.int32) + has_high.astype(jnp.int32))

    def copy(src, dst, slot, to):
        return pltpu.make_async_remote_copy(
            src_ref=src,
            dst_ref=dst,
            send_sem=send.at[slot],
            recv_sem=recv.at[slot],
            device_id={"span": to},
            device_id_type=pl.DeviceIdType.MESH,
        )

    up = [
        copy(win_hbm, win_low, 0, device + 1),
        copy(sh_hbm, sh_low, 1, device + 1),
        copy(b_hbm.at[pl.ds(CY - HALO, HALO)], low_raw, 2, device + 1),
    ]
    down = [
        copy(win_hbm, win_high, 3, device - 1),
        copy(sh_hbm, sh_high, 4, device - 1),
        copy(b_hbm.at[pl.ds(0, HALO)], high_raw, 5, device - 1),
    ]

    def exchange(up, down):
        @pl.when(has_high)
        def _():
            for c in up:
                c.start()

        @pl.when(has_low)
        def _():
            for c in down:
                c.start()

    def settle(up, down):
        @pl.when(has_high)
        def _():
            for c in up:
                c.wait_send()
            for c in down:
                c.wait_recv()

        @pl.when(has_low)
        def _():
            for c in down:
                c.wait_send()
            for c in up:
                c.wait_recv()

    exchange(up, down)

    tail = jnp.zeros((LANES - nz, nx), BF16)
    own_low, own_high = PAD_X // SUB, (PAD_X + nx) // SUB
    blank_low = jnp.zeros((own_low, SUB, LANES), BF16)
    blank_high = jnp.zeros((x_blocks - own_high, SUB, LANES), BF16)

    def turned(plane):
        return jnp.concatenate([plane, tail], axis=0).T

    def put(ref, at, plane):
        ref[at, :own_low] = blank_low
        ref[at, own_low:own_high] = plane.reshape(nx // SUB, SUB, LANES)
        ref[at, own_high:] = blank_high

    def put_second(at, plane):
        t = turned(plane)
        put(b_t.at[1], at, t)
        put(b_t.at[0], at, pltpu.roll(t, 1, 1))
        put(b_t.at[2], at, pltpu.roll(t, LANES - 1, 1))

    for c in range(parts):
        loads[2 * c].wait()
        loads[2 * c + 1].wait()

        def prepare(i, _):
            for k in range(2):
                y = c * PREP + 2 * i + k
                put_second(B_OFF + y, b_raw[y])
                put(a_t, A_OFF + y, turned(a_raw[y]))
            return 0

        lax.fori_loop(0, PREP // 2, prepare, 0)

    def blank(ref, begin, end):
        def one(y, _):
            ref[y] = jnp.zeros((x_blocks, SUB, LANES), BF16)
            return 0

        lax.fori_loop(begin, end, one, 0)

    @pl.when(no_low)
    def _():
        blank(a_t, 0, A_OFF)
        for g in range(3):
            blank(b_t.at[g], 0, B_OFF)
        for r in range(win.shape[0]):
            win_low[r] = 0
            for q in range(3):
                sh_low[q, r] = 0

    @pl.when(no_high)
    def _():
        blank(a_t, A_OFF + CY, A_PLANES)
        for g in range(3):
            blank(b_t.at[g], B_OFF + CY, B_PLANES)
        for r in range(win.shape[0]):
            win_high[r] = 0
            for q in range(3):
                sh_high[q, r] = 0

    settle(up, down)

    @pl.when(has_low)
    def _():
        for k in range(HALO):
            put_second(B_OFF - HALO + k, low_raw[k])

    @pl.when(has_high)
    def _():
        for k in range(HALO):
            put_second(B_OFF + CY + k, high_raw[k])

    def choose(wins, shs, lower, slot):
        count = jnp.int32(0)
        got = [jnp.int32(0)] * 4
        for r in range(win.shape[0]):
            node = wins[r]
            row = (node // GZX) % ROWS_TILE
            fits = (row < 2) if lower else (row >= 2)
            here = fits & (count == slot)
            count = count + fits.astype(jnp.int32)
            values = (node, shs[0, r], shs[1, r], shs[2, r])
            got = [jnp.where(here, v, g) for v, g in zip(values, got)]
        return got

    def edge(cond, own, other):
        return [jnp.where(cond, o, v) for o, v in zip(own, other)]

    def task(kind, slot):
        if kind == 0:
            return choose(win, sh, True, slot), 0, CY
        if kind == 1:
            return choose(win, sh, False, slot), 0, CY
        if kind == 2:
            who = edge(no_low, choose(win, sh, True, slot), choose(win_low, sh_low, False, slot))
            return who, jnp.where(no_low, -SPILL, 0), jnp.where(no_low, 0, CY)
        who = edge(no_high, choose(win, sh, False, slot), choose(win_high, sh_high, True, slot))
        return who, jnp.where(no_high, CY, 0), jnp.where(no_high, CY + SPILL, CY)

    a_first, a_last = jnp.where(no_low, -SPILL, 0), jnp.where(no_high, CY + SPILL, CY) - 1
    b_first = jnp.where(no_low, -SPILL, 0) - HALO
    b_last = jnp.where(no_high, CY + SPILL, CY) + HALO - 1

    def a_at(y):
        return jnp.minimum(jnp.maximum(y, a_first), a_last) + A_OFF

    def b_at(y):
        return jnp.minimum(jnp.maximum(y, b_first), b_last) + B_OFF

    def place(kind, slot):
        (node, dy, dz, dx), p0, p1 = task(kind, slot)
        yw = STRIDE * (node // GZX - ROWS_TILE * device) + STRIDE // 2 - HALF
        z0 = STRIDE * ((node % GZX) // GX) + STRIDE // 2 - HALF
        xa = STRIDE * (node % GX) + STRIDE // 2 - HALF + PAD_X
        xb = xa + dx - 1
        ya = jnp.maximum(yw, p0)
        yb = jnp.minimum(yw + W, p1)
        ny = jnp.maximum(yb - ya, 0)
        from_start, to_end = ya == yw, yb == yw + W
        xa0, xb0 = xa // SUB, xb // SUB
        xb4 = jnp.minimum(xb0 + XR // SUB, x_blocks - 1)
        off_a, off_b = xa - SUB * xa0, xb - SUB * xb0
        return ya, dy, dz, z0, ny, from_start, to_end, xa0, off_a, xb0, off_b, xb4

    def blocks(at, x0):
        return [at(x0 + k) for k in range(XR // SUB)]

    row = lax.broadcasted_iota(jnp.int32, (XR, LANES), 0)
    lane = lax.broadcasted_iota(jnp.int32, (XR, LANES), 1)

    def masks(z0, dz, off_a, off_b):
        z_in = ((lane - z0) & (LANES - 1)) < W
        x_in = (row >= off_a) & (row < off_a + W)
        zb_in = ((lane - z0 - dz + 1) & (LANES - 1)) < BW
        xb_in = ((row - off_b) & (XR - 1)) < BW
        return z_in, x_in, zb_in & xb_in

    def pivot(kind, slot):
        ya, dy, dz, z0, ny, _, _, xa0, off_a, xb0, off_b, _ = place(kind, slot)
        z_in, x_in, b_in = masks(z0, dz, off_a, off_b)
        y = a_at(ya + ny // 2)
        a = jnp.concatenate(blocks(lambda x: a_t[y, x], xa0), axis=0).astype(F32)
        y_b = b_at(ya + dy + ny // 2)
        b = jnp.concatenate(blocks(lambda x: b_t[1, y_b, x], xb0), axis=0).astype(F32)
        pa = jnp.sum(jnp.where(z_in & x_in, a, 0.0), keepdims=True) * (1.0 / (W * W))
        pb = jnp.sum(jnp.where(b_in, b, 0.0), keepdims=True) * (1.0 / (BW * BW))
        at = kind * SLOTS + slot
        pivots[at, :16, :] = jnp.broadcast_to(pa, (16, LANES)).astype(BF16)
        pivots[at, 16:, :] = jnp.broadcast_to(pb, (16, LANES)).astype(BF16)

    for kind in range(4):
        for slot in range(SLOTS):
            pivot(kind, slot)

    row_g = lax.broadcasted_iota(jnp.int32, (XR, 3 * XR), 0)
    col_g = lax.broadcasted_iota(jnp.int32, (XR, 3 * XR), 1) & (XR - 1)

    def tiled(v):
        return jnp.concatenate([v] * (XR // 16), axis=0)

    def add8(v):
        total = v[0:8]
        for k in range(1, XR // 8):
            total = total + v[8 * k : 8 * k + 8]
        return total

    def correlate(kind, planes, slot, _):
        ya, dy, dz, z0, ny, from_start, to_end, xa0, off_a, xb0, off_b, xb4 = place(kind, slot)
        at = kind * SLOTS + slot
        z_in, x_in, b_in = masks(z0, dz, off_a, off_b)
        zero = jnp.zeros((XR, LANES), BF16)
        keep_a = jnp.where(z_in & x_in, 1.0, 0.0).astype(BF16)
        ones_a = jnp.where(z_in & (row == XR - 1), 1.0, 0.0).astype(BF16)
        keep_b = jnp.where(b_in, 1.0, 0.0).astype(BF16)
        wrap = jnp.where(row[:16] < off_b, 1.0, 0.0).astype(BF16)
        stay = jnp.where(row[:16] < off_b, 0.0, 1.0).astype(BF16)
        pa = tiled(pivots[at, :16, :])
        pb = tiled(pivots[at, 16:, :])
        turn = dz & (LANES - 1)
        for k in (0, 1, planes + 2, planes + 3):
            a_s[k] = zero
        sums = [jnp.zeros((8, LANES), F32)] * 4

        def first(t):
            y = a_at(ya + t)
            raw = jnp.concatenate(blocks(lambda x: a_t[y, x], xa0), axis=0)
            valid = t < ny
            v = jnp.where(valid, (raw - pa) * keep_a, zero)
            x = v.astype(F32)
            sums[0] = sums[0] + add8(x)
            sums[1] = sums[1] + add8(x * x)
            v = v + jnp.where(valid, ones_a, zero)
            a_s[t + 2] = pltpu.roll(v, turn, 1)

        low_u = jnp.where(from_start, 0, 1)
        high_u = jnp.where(to_end, ny + 1, ny)
        some = ny > 0

        def second(u):
            y = b_at(ya + dy - 1 + u)
            got = []
            for g in range(3):
                t = blocks(lambda x: b_t[g, y, x], xb0)
                t[0] = t[0] * stay + b_t[g, y, xb4] * wrap
                v = jnp.concatenate(t, axis=0) - pb
                if g == 1:
                    use = some & (u >= low_u) & (u <= high_u)
                    x = (v * jnp.where(use, keep_b, zero)).astype(F32)
                    sums[2] = sums[2] + add8(x)
                    sums[3] = sums[3] + add8(x * x)
                got.append(v)
            return jnp.concatenate(got, axis=0)

        gram = jnp.zeros((3 * XR, 3 * XR), F32)
        done = 0
        begin = 0
        for size in sizes(planes):
            for t in range(done, min(begin + size, planes)):
                first(t)
            done = min(begin + size, planes)
            us = range(begin, begin + size)
            left = jnp.concatenate(
                [jnp.concatenate([a_s[u - f + 2] for u in us], axis=1) for f in range(3)], axis=0
            )
            right = jnp.concatenate([second(u) for u in us], axis=1)
            gram = gram + lax.dot_general(
                left, right, (((1,), (1,)), ((), ())), preferred_element_type=F32
            )
            begin += size

        gap = (col_g - row_g - (off_b - off_a)) & (XR - 1)
        real = row_g < XR - 1
        picks = [real & (gap == e) for e in range(3)]
        out_lines = []
        for f in range(3):
            block = gram[f * XR : (f + 1) * XR, :]
            for e in range(3):
                out_lines.append(jnp.sum(jnp.where(picks[e], block, 0.0), axis=0, keepdims=True))
        t_col = (col_g[:1] - off_b) & (XR - 1)
        for f in range(3):
            line = gram[(f + 1) * XR - 1 : (f + 1) * XR, :]
            for e in range(3):
                out_lines.append(jnp.where((t_col >= e) & (t_col < e + W), line, 0.0))
        out_lines.append(jnp.zeros((6, 3 * XR), F32))
        lines[at] = jnp.concatenate(out_lines, axis=0)
        for k in range(4):
            stats[at, k] = sums[k]
        return 0

    for kind, planes in enumerate((LOWER, W, SPILL, SPILL)):
        lax.fori_loop(0, SLOTS, functools.partial(correlate, kind, planes), 0)

    lane_p = lax.broadcasted_iota(jnp.int32, (80, LANES), 1)
    seg = lax.broadcasted_iota(jnp.int32, (24, 3 * XR), 1)
    table = jnp.zeros((80, LANES), F32)
    for kind in range(4):
        for slot in range(SLOTS):
            at = kind * SLOTS + slot
            _, _, _, _, ny, from_start, to_end, *_ = place(kind, slot)
            block = lines[at]
            columns = []
            for g in range(3):
                inside = (seg >= g * XR) & (seg < (g + 1) * XR)
                columns.append(jnp.sum(jnp.where(inside, block, 0.0), axis=1, keepdims=True))
            for k in range(4):
                columns.append(jnp.sum(stats[at, k], keepdims=True))
            columns.append(pivots[at, 0:1, 0:1].astype(F32))
            columns.append(pivots[at, 16:17, 0:1].astype(F32))
            nb = jnp.where(
                ny > 0, ny + from_start.astype(jnp.int32) + to_end.astype(jnp.int32), 0
            )
            columns.append(jnp.full((1, 1), (ny * (W * W)).astype(F32)))
            columns.append(jnp.full((1, 1), (nb * (BW * BW)).astype(F32)))
            column = jnp.concatenate(columns, axis=0)
            table = jnp.where(lane_p == at, column, table)
    mine[...] = table

    up = [copy(mine, low, 6, device + 1)]
    down = [copy(mine, high, 7, device - 1)]
    exchange(up, down)

    @pl.when(no_low)
    def _():
        low[...] = pltpu.roll(table, 4, 1)

    @pl.when(no_high)
    def _():
        high[...] = pltpu.roll(table, LANES - 4, 1)

    settle(up, down)

    lower, upper = low[...], high[...]
    other = jnp.where(
        lane_p < 4,
        pltpu.roll(lower, LANES - 12, 1),
        jnp.where(
            lane_p < 8,
            pltpu.roll(upper, LANES - 4, 1),
            jnp.where(lane_p < 12, pltpu.roll(lower, 4, 1), pltpu.roll(upper, 12, 1)),
        ),
    )
    both = (table, other)
    rows = [[p[72 + r : 73 + r] for r in range(8)] for p in both]
    mean_a = sum(s[0] + s[6] * s[4] for s in rows) / float(W) ** 3
    mean_b = sum(s[2] + s[7] * s[5] for s in rows) / float(BW) ** 3
    energy_a = jnp.zeros((1, LANES), F32)
    energy_b = jnp.zeros((1, LANES), F32)
    corr = [jnp.zeros((9, LANES), F32) for _ in range(3)]
    for p, s in zip(both, rows):
        da = s[4] - mean_a
        db = s[5] - mean_b
        energy_a += s[1] + 2.0 * da * s[0] + s[6] * da * da
        energy_b += s[3] + 2.0 * db * s[2] + s[7] * db * db
        rest = db * s[0] + s[6] * da * db
        for g in range(3):
            base = 24 * g
            corr[g] = corr[g] + (p[base : base + 9] + da * p[base + 9 : base + 18] + rest)
    energy_a = energy_a / float(W) ** 3
    energy_b = energy_b / float(BW) ** 3
    normaliser = float(W) ** 3 * jnp.sqrt((energy_a + EPSILON) * (energy_b + EPSILON))
    weights = [jnp.exp(SHARP * (c / normaliser)) for c in corr]
    totals = [jnp.sum(v, axis=0, keepdims=True) for v in weights]
    total = totals[0] + totals[1] + totals[2]
    every = weights[0] + weights[1] + weights[2]
    row_9 = lax.broadcasted_iota(jnp.int32, (9, LANES), 0)
    lag_y = jnp.where(row_9 >= 6, 1.0, jnp.where(row_9 >= 3, 0.0, -1.0))
    row_x = row_9 - jnp.where(row_9 >= 6, 6, jnp.where(row_9 >= 3, 3, 0))
    lag_x = row_x.astype(F32) - 1.0
    along = (
        jnp.sum(every * lag_y, axis=0, keepdims=True) / total,
        (totals[2] - totals[0]) / total,
        jnp.sum(every * lag_x, axis=0, keepdims=True) / total,
    )
    row_f = lax.broadcasted_iota(jnp.int32, (8, GZX), 0)
    lane_f = lax.broadcasted_iota(jnp.int32, (8, GZX), 1)
    fields = [jnp.zeros((8, GZX), F32) for _ in range(3)]
    for kind in range(4):
        for slot in range(SLOTS):
            at = kind * SLOTS + slot
            node = task(kind, slot)[0][0]
            at_row = node // GZX - ROWS_TILE * device + 1
            if kind == 2:
                at_row = jnp.where(no_low, -1, at_row)
            if kind == 3:
                at_row = jnp.where(no_high, -1, at_row)
            hit = (row_f == at_row) & (lane_f == node % GZX)
            for c in range(3):
                fields[c] = jnp.where(hit, along[c][:, at : at + 1], fields[c])
    deep = lane_f // GX
    stream = lane_f % GX
    for c in range(3):
        u = fields[c]
        near = (
            jnp.where(deep < GZ - 1, pltpu.roll(u, GZX - GX, 1), 0.0)
            + jnp.where(deep > 0, pltpu.roll(u, GX, 1), 0.0)
            + jnp.where(stream < GX - 1, pltpu.roll(u, GZX - 1, 1), 0.0)
            + jnp.where(stream > 0, pltpu.roll(u, 1, 1), 0.0)
        )
        near = near + pltpu.roll(u, 7, 0) + pltpu.roll(u, 1, 0)
        smooth = 0.4 * u + 0.1 * near
        out[c] = smooth[1 : 1 + ROWS_TILE]


def shards(first_exposure, second_exposure, windows, shifts):
    n = lax.axis_size("span")
    nz, nx = first_exposure.shape[1:]
    x_blocks = (PAD_X + nx + PAD_X) // SUB
    smem = pl.BlockSpec(memory_space=pltpu.SMEM)
    hbm = pl.BlockSpec(memory_space=pltpu.HBM)
    anywhere = pl.BlockSpec(memory_space=pl.ANY)
    return pl.pallas_call(
        functools.partial(kernel, n),
        name="update",
        out_shape=jax.ShapeDtypeStruct((3, CY // STRIDE, GZX), F32),
        in_specs=[smem, smem, anywhere, anywhere, hbm, hbm],
        out_specs=pl.BlockSpec(memory_space=pltpu.VMEM),
        scratch_shapes=[
            pltpu.VMEM((CY, nz, nx), BF16),
            pltpu.VMEM((CY, nz, nx), BF16),
            pltpu.VMEM((HALO, nz, nx), BF16),
            pltpu.VMEM((HALO, nz, nx), BF16),
            pltpu.SMEM(windows.shape, jnp.int32),
            pltpu.SMEM(windows.shape, jnp.int32),
            pltpu.SMEM(shifts.shape, jnp.int32),
            pltpu.SMEM(shifts.shape, jnp.int32),
            pltpu.VMEM((A_PLANES, x_blocks, SUB, LANES), BF16),
            pltpu.VMEM((3, B_PLANES, x_blocks, SUB, LANES), BF16),
            pltpu.VMEM((W + 4, XR, LANES), BF16),
            pltpu.VMEM((TASKS, 32, LANES), BF16),
            pltpu.VMEM((TASKS, 24, 3 * XR), F32),
            pltpu.VMEM((TASKS, 4, 8, LANES), F32),
            pltpu.VMEM((80, LANES), F32),
            pltpu.VMEM((80, LANES), F32),
            pltpu.VMEM((80, LANES), F32),
            pltpu.SemaphoreType.DMA((8,)),
            pltpu.SemaphoreType.DMA((8,)),
            pltpu.SemaphoreType.DMA((2 * (CY // PREP),)),
        ],
        compiler_params=pltpu.CompilerParams(
            collective_id=0, has_side_effects=True, vmem_limit_bytes=50 << 20
        ),
    )(windows, shifts, windows, shifts, first_exposure, second_exposure)


def solution(mesh):
    in_specs = (
        P(("grp", "span"), None, None),
        P(("grp", "span"), None, None),
        P(("grp", "span")),
        P(None, ("grp", "span")),
    )
    out_specs = P(None, ("grp", "span"), None)
    return jax.shard_map(shards, mesh=mesh, in_specs=in_specs, out_specs=out_specs, check_vma=False)
```

```python
import functools

import jax
import jax.numpy as jnp
from jax import lax
from jax.experimental import pallas as pl
from jax.experimental.pallas import tpu as pltpu
from jax.sharding import PartitionSpec as P

W = 48
STRIDE = 12
DYM = 3
GZ = 8
GX = 16
GZX = 128
HALO = DYM + 1
HALF = W // 2
BW = W + 2
ROWS_TILE = 5
CY = STRIDE * ROWS_TILE
SPILL = 18
LOWER = 42
SLOTS = 4
TASKS = 16

SHARP = 80.0
EPSILON = 1e-06

F32 = jnp.float32
BF16 = jnp.bfloat16

PAD_X = 32
XR = 64
LANES = 128
SUB = 16
A_OFF = SPILL
A_PLANES = SPILL + CY + SPILL
B_OFF = SPILL + HALO
B_PLANES = B_OFF + CY + B_OFF
CHUNK = 10
PLANES = (LOWER, W, SPILL, SPILL)
VMEM_BYTES = 62 << 20
PREP = 12
STEP = 6
LINES = 28


def sizes(n):
    total = n + 2
    out = []
    while total > 0:
        out.append(min(CHUNK, total))
        total -= CHUNK
    return out


def kernel(
    n, win_hbm, sh_hbm, a_hbm, b_hbm, out,
    win, sh, a_raw, b_raw, low_raw, high_raw, win_low, win_high, sh_low, sh_high,
    a_t, b_t, s0, s1, s2, s3, pivots, sum_a, sum_b, lines, mine, low, high, send, recv, sems,
):
    nz, nx = a_hbm.shape[1], a_hbm.shape[2]
    x_blocks = a_t.shape[1]
    device = lax.axis_index("span")
    last = n - 1
    has_low, has_high = device > 0, device < last
    no_low, no_high = device == 0, device == last
    parts = CY // PREP
    loads = []
    for c in range(parts):
        rows = pl.ds(c * PREP, PREP)
        loads.append(pltpu.make_async_copy(b_hbm.at[rows], b_raw.at[rows], sems.at[2 * c]))
        loads.append(pltpu.make_async_copy(a_hbm.at[rows], a_raw.at[rows], sems.at[2 * c + 1]))
    own = [
        pltpu.make_async_copy(win_hbm, win, sems.at[2 * parts]),
        pltpu.make_async_copy(sh_hbm, sh, sems.at[2 * parts + 1]),
    ]
    for load in own + loads:
        load.start()

    barrier = pltpu.get_barrier_semaphore()

    def greet(to):
        pl.semaphore_signal(
            barrier, inc=1, device_id={"span": to}, device_id_type=pl.DeviceIdType.MESH
        )

    @pl.when(has_low)
    def _():
        greet(device - 1)

    @pl.when(has_high)
    def _():
        greet(device + 1)

    pl.semaphore_wait(barrier, has_low.astype(jnp.int32) + has_high.astype(jnp.int32))

    def copy(src, dst, slot, to):
        return pltpu.make_async_remote_copy(
            src_ref=src,
            dst_ref=dst,
            send_sem=send.at[slot],
            recv_sem=recv.at[slot],
            device_id={"span": to},
            device_id_type=pl.DeviceIdType.MESH,
        )

    up = [
        copy(win_hbm, win_low, 0, device + 1),
        copy(sh_hbm, sh_low, 1, device + 1),
        copy(b_hbm.at[pl.ds(CY - HALO, HALO)], low_raw, 2, device + 1),
    ]
    down = [
        copy(win_hbm, win_high, 3, device - 1),
        copy(sh_hbm, sh_high, 4, device - 1),
        copy(b_hbm.at[pl.ds(0, HALO)], high_raw, 5, device - 1),
    ]

    def exchange(up, down):
        @pl.when(has_high)
        def _():
            for c in up:
                c.start()

        @pl.when(has_low)
        def _():
            for c in down:
                c.start()

    def settle(up, down):
        @pl.when(has_high)
        def _():
            for c in up:
                c.wait_send()
            for c in down:
                c.wait_recv()

        @pl.when(has_low)
        def _():
            for c in down:
                c.wait_send()
            for c in up:
                c.wait_recv()

    exchange(up, down)

    tail = jnp.zeros((LANES - nz, nx), BF16)
    own_low, own_high = PAD_X // SUB, (PAD_X + nx) // SUB
    blank_low = jnp.zeros((own_low, SUB, LANES), BF16)
    blank_high = jnp.zeros((x_blocks - own_high, SUB, LANES), BF16)

    def turned(plane):
        return jnp.concatenate([plane, tail], axis=0).T

    def put(ref, at, plane):
        ref[at, :own_low] = blank_low
        ref[at, own_low:own_high] = plane.reshape(nx // SUB, SUB, LANES)
        ref[at, own_high:] = blank_high

    def put_second(at, plane):
        t = turned(plane)
        put(b_t.at[1], at, t)
        put(b_t.at[0], at, pltpu.roll(t, 1, 1))
        put(b_t.at[2], at, pltpu.roll(t, LANES - 1, 1))

    x_own = nx // SUB

    def level(plane):
        return jnp.sum(plane.astype(F32), keepdims=True) * (1.0 / (nz * nx))

    def add_up(totals, plane, base, sign):
        x = plane.astype(F32) - base
        return [totals[0] + sign * x, totals[1] + sign * (x * x)]

    for c in range(parts):
        loads[2 * c].wait()
        loads[2 * c + 1].wait()
        if c == 0:
            base_a, base_b = level(a_raw[0]), level(b_raw[0])
            for k in range(2):
                sum_a[k, 0] = jnp.zeros((x_own, SUB, LANES), F32)
                sum_b[k, HALO] = jnp.zeros((x_own, SUB, LANES), F32)

        def prepare(i, _):
            y = c * PREP + i * STEP
            group = c * (PREP // STEP) + i
            for k in range(STEP):
                put_second(B_OFF + y + k, b_raw[y + k])
                put(a_t, A_OFF + y + k, turned(a_raw[y + k]))
            for x in range(x_own):
                totals = [sum_b[0, HALO + y, x], sum_b[1, HALO + y, x]]
                for k in range(STEP):
                    totals = add_up(totals, b_t[1, B_OFF + y + k, own_low + x], base_b, 1.0)
                    sum_b[0, HALO + y + k + 1, x] = totals[0]
                    sum_b[1, HALO + y + k + 1, x] = totals[1]
                totals = [sum_a[0, group, x], sum_a[1, group, x]]
                for k in range(STEP):
                    totals = add_up(totals, a_t[A_OFF + y + k, own_low + x], base_a, 1.0)
                sum_a[0, group + 1, x] = totals[0]
                sum_a[1, group + 1, x] = totals[1]
            return 0

        lax.fori_loop(0, PREP // STEP, prepare, 0)

    def blank(ref, begin, end):
        def one(y, _):
            ref[y] = jnp.zeros((x_blocks, SUB, LANES), BF16)
            return 0

        lax.fori_loop(begin, end, one, 0)

    @pl.when(no_low)
    def _():
        blank(a_t, 0, A_OFF)
        for g in range(3):
            blank(b_t.at[g], 0, B_OFF)
        for r in range(win.shape[0]):
            win_low[r] = 0
            for q in range(3):
                sh_low[q, r] = 0

    @pl.when(no_high)
    def _():
        blank(a_t, A_OFF + CY, A_PLANES)
        for g in range(3):
            blank(b_t.at[g], B_OFF + CY, B_PLANES)
        for r in range(win.shape[0]):
            win_high[r] = 0
            for q in range(3):
                sh_high[q, r] = 0

    for load in own:
        load.wait()
    settle(up[:2], down[:2])

    def choose(wins, shs, lower, slot):
        count = jnp.int32(0)
        got = [jnp.int32(0)] * 4
        for r in range(win.shape[0]):
            node = wins[r]
            row = (node // GZX) % ROWS_TILE
            fits = (row < 2) if lower else (row >= 2)
            here = fits & (count == slot)
            count = count + fits.astype(jnp.int32)
            values = (node, shs[0, r], shs[1, r], shs[2, r])
            got = [jnp.where(here, v, g) for v, g in zip(values, got)]
        return got

    def edge(cond, own, other):
        return [jnp.where(cond, o, v) for o, v in zip(own, other)]

    def task(kind, slot):
        if kind == 0:
            return choose(win, sh, True, slot), 0, CY
        if kind == 1:
            return choose(win, sh, False, slot), 0, CY
        if kind == 2:
            who = edge(no_low, choose(win, sh, True, slot), choose(win_low, sh_low, False, slot))
            return who, jnp.where(no_low, -SPILL, 0), jnp.where(no_low, 0, CY)
        who = edge(no_high, choose(win, sh, False, slot), choose(win_high, sh_high, True, slot))
        return who, jnp.where(no_high, CY, 0), jnp.where(no_high, CY + SPILL, CY)

    a_first, a_last = jnp.where(no_low, -SPILL, 0), jnp.where(no_high, CY + SPILL, CY) - 1
    b_first = jnp.where(no_low, -SPILL, 0) - HALO
    b_last = jnp.where(no_high, CY + SPILL, CY) + HALO - 1

    def a_at(y):
        return jnp.minimum(jnp.maximum(y, a_first), a_last) + A_OFF

    def b_at(y):
        return jnp.minimum(jnp.maximum(y, b_first), b_last) + B_OFF

    def place(kind, slot):
        (node, dy, dz, dx), p0, p1 = task(kind, slot)
        yw = STRIDE * (node // GZX - ROWS_TILE * device) + STRIDE // 2 - HALF
        z0 = STRIDE * ((node % GZX) // GX) + STRIDE // 2 - HALF
        xa = STRIDE * (node % GX) + STRIDE // 2 - HALF + PAD_X
        xb = xa + dx - 1
        ya = jnp.maximum(yw, p0)
        yb = jnp.minimum(yw + W, p1)
        ny = jnp.maximum(yb - ya, 0)
        from_start, to_end = ya == yw, yb == yw + W
        xa0, xb0 = xa // SUB, xb // SUB
        xb4 = jnp.minimum(xb0 + XR // SUB, x_blocks - 1)
        off_a, off_b = xa - SUB * xa0, xb - SUB * xb0
        return ya, dy, dz, z0, ny, from_start, to_end, xa0, off_a, xb0, off_b, xb4

    def blocks(at, x0):
        return [at(x0 + k) for k in range(XR // SUB)]

    row = lax.broadcasted_iota(jnp.int32, (XR, LANES), 0)
    lane = lax.broadcasted_iota(jnp.int32, (XR, LANES), 1)

    def masks(z0, dz, off_a, off_b):
        z_in = ((lane - z0) & (LANES - 1)) < W
        x_in = (row >= off_a) & (row < off_a + W)
        zb_in = ((lane - z0 - dz + 1) & (LANES - 1)) < BW
        xb_in = ((row - off_b) & (XR - 1)) < BW
        return z_in, x_in, zb_in & xb_in

    def pivot(kind, slot):
        ya, dy, dz, z0, ny, _, _, xa0, off_a, xb0, off_b, _ = place(kind, slot)
        z_in, x_in, b_in = masks(z0, dz, off_a, off_b)
        y = a_at(ya + ny // 2)
        a = jnp.concatenate(blocks(lambda x: a_t[y, x], xa0), axis=0).astype(F32)
        y_b = jnp.minimum(jnp.maximum(ya + dy + ny // 2, 0), CY - 1) + B_OFF
        b = jnp.concatenate(blocks(lambda x: b_t[1, y_b, x], xb0), axis=0).astype(F32)
        pa = jnp.sum(jnp.where(z_in & x_in, a, 0.0), keepdims=True) * (1.0 / (W * W))
        pb = jnp.sum(jnp.where(b_in, b, 0.0), keepdims=True) * (1.0 / (BW * BW))
        at = kind * SLOTS + slot
        pivots[at, :16, :] = jnp.broadcast_to(pa, (16, LANES)).astype(BF16)
        pivots[at, 16:, :] = jnp.broadcast_to(pb, (16, LANES)).astype(BF16)

    for kind in range(4):
        for slot in range(SLOTS):
            pivot(kind, slot)

    settle(up[2:], down[2:])

    @pl.when(has_low)
    def _():
        for k in range(HALO):
            put_second(B_OFF - HALO + k, low_raw[k])
        for x in range(x_own):
            totals = [sum_b[0, HALO, x], sum_b[1, HALO, x]]
            for k in range(HALO):
                plane = b_t[1, B_OFF - 1 - k, own_low + x]
                totals = add_up(totals, plane, base_b, -1.0)
                sum_b[0, HALO - 1 - k, x] = totals[0]
                sum_b[1, HALO - 1 - k, x] = totals[1]

    @pl.when(has_high)
    def _():
        for k in range(HALO):
            put_second(B_OFF + CY + k, high_raw[k])
        for x in range(x_own):
            totals = [sum_b[0, HALO + CY, x], sum_b[1, HALO + CY, x]]
            for k in range(HALO):
                plane = b_t[1, B_OFF + CY + k, own_low + x]
                totals = add_up(totals, plane, base_b, 1.0)
                sum_b[0, HALO + CY + k + 1, x] = totals[0]
                sum_b[1, HALO + CY + k + 1, x] = totals[1]

    parts_s = (s0, s1, s2, s3)
    row_g = lax.broadcasted_iota(jnp.int32, (XR, 3 * XR), 0)
    col_g = lax.broadcasted_iota(jnp.int32, (XR, 3 * XR), 1) & (XR - 1)

    def tiled(v):
        return jnp.concatenate([v] * (XR // 16), axis=0)

    lane_1 = lax.broadcasted_iota(jnp.int32, (1, LANES), 1)
    row_b = lax.broadcasted_iota(jnp.int32, (XR + SUB, LANES), 0)
    lane_b = lax.broadcasted_iota(jnp.int32, (XR + SUB, LANES), 1)
    b_lo, b_hi = jnp.where(no_low, 0, -HALO), jnp.where(no_high, CY, CY + HALO)

    def clip(v, lo, hi):
        return jnp.minimum(jnp.maximum(v, lo), hi)

    def part_sums(ref, begin, end, x0, count, keep, base, total, held):
        outside = (total - held).astype(F32)
        got = []
        for k in range(2):
            rows = []
            for b in range(count):
                x = clip(x0 + b - own_low, 0, x_own - 1)
                rows.append(ref[k, end, x] - ref[k, begin, x])
            v = jnp.where(keep, jnp.concatenate(rows, axis=0), 0.0)
            extra = base * base if k else -base
            line = jnp.sum(v, axis=0, keepdims=True)
            got.append(line + jnp.where(lane_1 == 0, extra * outside, 0.0))
        return got

    def wide(line):
        line = line + pltpu.roll(line, XR, 1)
        return jnp.concatenate([line, line[:, :XR]], axis=1)

    def only(value):
        return jnp.where(lane_1 == 0, value, 0.0)

    def correlate(kind, planes, slot):
        a_s = parts_s[kind]
        ya, dy, dz, z0, ny, from_start, to_end, xa0, off_a, xb0, off_b, xb4 = place(kind, slot)
        at = kind * SLOTS + slot
        z_in, x_in, _ = masks(z0, dz, off_a, off_b)
        zero = jnp.zeros((XR, LANES), BF16)
        keep_a = jnp.where(z_in & x_in, 1.0, 0.0).astype(BF16)
        ones_a = jnp.where(z_in & (row == XR - 1), 1.0, 0.0).astype(BF16)
        wrap = jnp.where(row[:16] < off_b, 1.0, 0.0).astype(BF16)
        stay = jnp.where(row[:16] < off_b, 0.0, 1.0).astype(BF16)
        pa = tiled(pivots[at, :16, :])
        pb = tiled(pivots[at, 16:, :])
        turn = dz & (LANES - 1)
        for k in (0, 1, planes + 2, planes + 3):
            a_s[k] = zero

        def first(t):
            y = a_at(ya + t)
            raw = jnp.concatenate(blocks(lambda x: a_t[y, x], xa0), axis=0)
            valid = t < ny
            v = jnp.where(valid, (raw - pa) * keep_a + ones_a, zero)
            a_s[t + 2] = pltpu.roll(v, turn, 1)

        some = ny > 0
        first_x, first_b = SUB * xa0 - PAD_X, SUB * xb0 - PAD_X
        y0, y1 = clip(ya, 0, CY), clip(ya + ny, 0, CY)
        rows_in = clip(first_x + off_a + W, 0, nx) - clip(first_x + off_a, 0, nx)
        n_a = ny * (W * W)
        stats = part_sums(
            sum_a, y0 // STEP, y1 // STEP, xa0, XR // SUB,
            z_in & x_in & (row + first_x >= 0) & (row + first_x < nx),
            base_a, n_a, (y1 - y0) * rows_in * W,
        )
        v0 = ya + dy - jnp.where(from_start, 1, 0)
        v1 = ya + dy + ny + jnp.where(to_end, 1, 0)
        v1 = jnp.where(some, v1, v0)
        n_b = (v1 - v0) * (BW * BW)
        v0, v1 = clip(v0, b_lo, b_hi), clip(v1, b_lo, b_hi)
        rows_in = clip(first_b + off_b + BW, 0, nx) - clip(first_b + off_b, 0, nx)
        stats += part_sums(
            sum_b, HALO + v0, HALO + v1, xb0, XR // SUB + 1,
            (((lane_b - z0 - dz + 1) & (LANES - 1)) < BW)
            & (row_b >= off_b) & (row_b < off_b + BW)
            & (row_b + first_b >= 0) & (row_b + first_b < nx),
            base_b, n_b, (v1 - v0) * rows_in * BW,
        )
        stats += [
            only(pivots[at, 0:1, 0:1].astype(F32)),
            only(pivots[at, 16:17, 0:1].astype(F32)),
            only(n_a.astype(F32)),
            only(n_b.astype(F32)),
            only(base_a),
            only(base_b),
        ]
        for k, line in enumerate(stats):
            lines[18 + k, pl.ds(at, 1), :] = wide(line)

        def second(u):
            y = b_at(ya + dy - 1 + u)
            got = []
            for g in range(3):
                t = blocks(lambda x: b_t[g, y, x], xb0)
                t[0] = t[0] * stay + b_t[g, y, xb4] * wrap
                v = jnp.concatenate(t, axis=0) - pb
                got.append(v)
            return jnp.concatenate(got, axis=0)

        gram = jnp.zeros((3 * XR, 3 * XR), F32)
        done = 0
        begin = 0
        for size in sizes(planes):
            for t in range(done, min(begin + size, planes)):
                first(t)
            done = min(begin + size, planes)
            us = range(begin, begin + size)
            left = jnp.concatenate(
                [jnp.concatenate([a_s[u - f + 2] for u in us], axis=1) for f in range(3)], axis=0
            )
            right = jnp.concatenate([second(u) for u in us], axis=1)
            gram = gram + lax.dot_general(
                left, right, (((1,), (1,)), ((), ())), preferred_element_type=F32
            )
            begin += size

        gap = (col_g - row_g - (off_b - off_a)) & (XR - 1)
        real = row_g < XR - 1
        picks = [real & (gap == e) for e in range(3)]
        out_lines = []
        for f in range(3):
            block = gram[f * XR : (f + 1) * XR, :]
            for e in range(3):
                out_lines.append(jnp.sum(jnp.where(picks[e], block, 0.0), axis=0, keepdims=True))
        t_col = (col_g[:1] - off_b) & (XR - 1)
        for f in range(3):
            line = gram[(f + 1) * XR - 1 : (f + 1) * XR, :]
            for e in range(3):
                out_lines.append(jnp.where((t_col >= e) & (t_col < e + W), line, 0.0))
        for q, line in enumerate(out_lines):
            lines[q, pl.ds(at, 1), :] = line

    def every_kind(slot, _):
        for kind, planes in enumerate(PLANES):
            correlate(kind, planes, slot)
        return 0

    lax.fori_loop(0, SLOTS, every_kind, 0)

    seg = lax.broadcasted_iota(jnp.int32, (8, 3 * XR), 0)
    seg_lane = lax.broadcasted_iota(jnp.int32, (8, 3 * XR), 1)
    select = jnp.where(seg_lane // XR == seg, 1.0, 0.0)
    table = lax.dot_general(
        select,
        lines[...].reshape(LINES * TASKS, 3 * XR),
        (((1,), (1,)), ((), ())),
        precision=lax.Precision.HIGHEST,
        preferred_element_type=F32,
    )
    table = jnp.concatenate([table, jnp.zeros((8, 4 * LANES - LINES * TASKS), F32)], axis=1)
    mine[...] = table

    def turn_lanes(v, by):
        pieces = [v[:, k * LANES : (k + 1) * LANES] for k in range(4)]
        return jnp.concatenate([pltpu.roll(p, by, 1) for p in pieces], axis=1)

    up = [copy(mine, low, 6, device + 1)]
    down = [copy(mine, high, 7, device - 1)]
    exchange(up, down)

    @pl.when(no_low)
    def _():
        low[...] = turn_lanes(mine[...], 4)

    @pl.when(no_high)
    def _():
        high[...] = turn_lanes(mine[...], LANES - 4)

    settle(up, down)

    lower, upper = low[...], high[...]
    task_lane = lax.broadcasted_iota(jnp.int32, (8, 4 * LANES), 1) & (TASKS - 1)
    other = jnp.where(
        task_lane < 4,
        turn_lanes(lower, LANES - 12),
        jnp.where(
            task_lane < 8,
            turn_lanes(upper, LANES - 4),
            jnp.where(task_lane < 12, turn_lanes(lower, 4), turn_lanes(upper, 12)),
        ),
    )

    def spread(v):
        got = []
        for q in range(LINES):
            piece = v[:, q // 8 * LANES : (q // 8 + 1) * LANES]
            by = (LANES - TASKS * (q % 8)) % LANES
            got.append(pltpu.roll(piece, by, 1) if by else piece)
        return got

    both = [spread(mine[...]), spread(other)]
    mean_a = sum(p[18] + p[24] * p[26] for p in both) / float(W) ** 3
    mean_b = sum(p[20] + p[25] * p[27] for p in both) / float(BW) ** 3
    energy_a = jnp.zeros((8, LANES), F32)
    energy_b = jnp.zeros((8, LANES), F32)
    corr = [jnp.zeros((8, LANES), F32)] * 9
    for p in both:
        da, db = p[26] - mean_a, p[27] - mean_b
        energy_a += p[19] + 2.0 * da * p[18] + p[24] * da * da
        energy_b += p[21] + 2.0 * db * p[20] + p[25] * db * db
        da, db = p[22] - mean_a, p[23] - mean_b
        rest = db * (p[18] + p[24] * (p[26] - p[22])) + p[24] * da * db
        corr = [v + (p[q] + da * p[9 + q] + rest) for q, v in enumerate(corr)]
    energy_a = energy_a / float(W) ** 3
    energy_b = energy_b / float(BW) ** 3
    normaliser = float(W) ** 3 * jnp.sqrt((energy_a + EPSILON) * (energy_b + EPSILON))
    row_s = lax.broadcasted_iota(jnp.int32, (8, LANES), 0)
    weights = [jnp.where(row_s < 3, jnp.exp(SHARP * (c / normaliser)), 0.0) for c in corr]
    by_z = sum(weights)
    by_y = sum(weights[6:]) - sum(weights[:3])
    by_x = sum(weights[2::3]) - sum(weights[0::3])
    total = jnp.sum(by_z, axis=0, keepdims=True)
    along = (
        jnp.sum(by_y, axis=0, keepdims=True) / total,
        (by_z[2:3] - by_z[0:1]) / total,
        jnp.sum(by_x, axis=0, keepdims=True) / total,
    )
    row_f = lax.broadcasted_iota(jnp.int32, (8, GZX), 0)
    lane_f = lax.broadcasted_iota(jnp.int32, (8, GZX), 1)
    fields = [jnp.zeros((8, GZX), F32) for _ in range(3)]
    for kind in range(4):
        for slot in range(SLOTS):
            at = kind * SLOTS + slot
            node = task(kind, slot)[0][0]
            at_row = node // GZX - ROWS_TILE * device + 1
            if kind == 2:
                at_row = jnp.where(no_low, -1, at_row)
            if kind == 3:
                at_row = jnp.where(no_high, -1, at_row)
            hit = (row_f == at_row) & (lane_f == node % GZX)
            for c in range(3):
                fields[c] = jnp.where(hit, along[c][:, at : at + 1], fields[c])
    deep = lane_f // GX
    stream = lane_f % GX
    for c in range(3):
        u = fields[c]
        near = (
            jnp.where(deep < GZ - 1, pltpu.roll(u, GZX - GX, 1), 0.0)
            + jnp.where(deep > 0, pltpu.roll(u, GX, 1), 0.0)
            + jnp.where(stream < GX - 1, pltpu.roll(u, GZX - 1, 1), 0.0)
            + jnp.where(stream > 0, pltpu.roll(u, 1, 1), 0.0)
        )
        near = near + pltpu.roll(u, 7, 0) + pltpu.roll(u, 1, 0)
        smooth = 0.4 * u + 0.1 * near
        out[c] = smooth[1 : 1 + ROWS_TILE]


def shards(first_exposure, second_exposure, windows, shifts):
    n = lax.axis_size("span")
    nz, nx = first_exposure.shape[1:]
    x_blocks = (PAD_X + nx + PAD_X) // SUB
    hbm = pl.BlockSpec(memory_space=pltpu.HBM)
    return pl.pallas_call(
        functools.partial(kernel, n),
        name="update",
        out_shape=jax.ShapeDtypeStruct((3, CY // STRIDE, GZX), F32),
        in_specs=[hbm] * 4,
        out_specs=pl.BlockSpec(memory_space=pltpu.VMEM),
        scratch_shapes=[
            pltpu.SMEM(windows.shape, jnp.int32),
            pltpu.SMEM(shifts.shape, jnp.int32),
            pltpu.VMEM((CY, nz, nx), BF16),
            pltpu.VMEM((CY, nz, nx), BF16),
            pltpu.VMEM((HALO, nz, nx), BF16),
            pltpu.VMEM((HALO, nz, nx), BF16),
            pltpu.SMEM(windows.shape, jnp.int32),
            pltpu.SMEM(windows.shape, jnp.int32),
            pltpu.SMEM(shifts.shape, jnp.int32),
            pltpu.SMEM(shifts.shape, jnp.int32),
            pltpu.VMEM((A_PLANES, x_blocks, SUB, LANES), BF16),
            pltpu.VMEM((3, B_PLANES, x_blocks, SUB, LANES), BF16),
            *(pltpu.VMEM((p + 4, XR, LANES), BF16) for p in PLANES),
            pltpu.VMEM((TASKS, 32, LANES), BF16),
            pltpu.VMEM((2, CY // STEP + 1, nx // SUB, SUB, LANES), F32),
            pltpu.VMEM((2, CY + 2 * HALO + 1, nx // SUB, SUB, LANES), F32),
            pltpu.VMEM((LINES, TASKS, 3 * XR), F32),
            pltpu.VMEM((8, 4 * LANES), F32),
            pltpu.VMEM((8, 4 * LANES), F32),
            pltpu.VMEM((8, 4 * LANES), F32),
            pltpu.SemaphoreType.DMA((8,)),
            pltpu.SemaphoreType.DMA((8,)),
            pltpu.SemaphoreType.DMA((2 * (CY // PREP) + 2,)),
        ],
        compiler_params=pltpu.CompilerParams(
            collective_id=0, has_side_effects=True, vmem_limit_bytes=VMEM_BYTES
        ),
    )(windows, shifts, first_exposure, second_exposure)


def solution(mesh):
    in_specs = (
        P(("grp", "span"), None, None),
        P(("grp", "span"), None, None),
        P(("grp", "span")),
        P(None, ("grp", "span")),
    )
    out_specs = P(None, ("grp", "span"), None)
    return jax.shard_map(shards, mesh=mesh, in_specs=in_specs, out_specs=out_specs, check_vma=False)
```

```python
import functools

import jax
import jax.numpy as jnp
from jax import lax
from jax.experimental import pallas as pl
from jax.experimental.pallas import tpu as pltpu
from jax.sharding import PartitionSpec as P

W = 48
STRIDE = 12
DYM = 3
GZ = 8
GX = 16
GZX = 128
HALO = DYM + 1
HALF = W // 2
BW = W + 2
ROWS_TILE = 5
CY = STRIDE * ROWS_TILE
SPILL = 18
LOWER = 42
LEAST = 30
SLOTS = 4
TASKS = 16

SHARP = 80.0
EPSILON = 1e-06

F32 = jnp.float32
BF16 = jnp.bfloat16

PAD_X = 32
XR = 64
LANES = 128
SUB = 16
A_OFF = SPILL
A_PLANES = SPILL + CY + SPILL
B_OFF = SPILL + HALO
B_PLANES = B_OFF + CY + B_OFF
CHUNK = 10
PLANES = (LOWER, W, SPILL, SPILL)
VMEM_BYTES = 62 << 20
PREP = 12
STEP = 6
LINES = 27


def sizes(n):
    total = n + 2
    out = []
    while total > 0:
        out.append(min(CHUNK, total))
        total -= CHUNK
    return out


def kernel(
    n, win_hbm, sh_hbm, a_hbm, b_hbm, out,
    win, sh, a_raw, b_raw, low_raw, high_raw, win_low, win_high, sh_low, sh_high,
    a_t, b_t, s0, s1, s2, s3, pivots, sum_a, sum_b, lines, mine, low, high, send, recv, sems,
):
    nz, nx = a_hbm.shape[1], a_hbm.shape[2]
    x_blocks = (PAD_X + nx + PAD_X) // SUB
    device = lax.axis_index("span")
    last = n - 1
    has_low, has_high = device > 0, device < last
    no_low, no_high = device == 0, device == last
    parts = CY // PREP
    loads = []
    for c in range(parts):
        rows = pl.ds(c * PREP, PREP)
        loads.append(pltpu.make_async_copy(b_hbm.at[rows], b_raw.at[rows], sems.at[2 * c]))
        loads.append(pltpu.make_async_copy(a_hbm.at[rows], a_raw.at[rows], sems.at[2 * c + 1]))
    own = [
        pltpu.make_async_copy(win_hbm, win, sems.at[2 * parts]),
        pltpu.make_async_copy(sh_hbm, sh, sems.at[2 * parts + 1]),
    ]
    for load in own + loads:
        load.start()

    barrier = pltpu.get_barrier_semaphore()

    def greet(to):
        pl.semaphore_signal(
            barrier, inc=1, device_id={"span": to}, device_id_type=pl.DeviceIdType.MESH
        )

    @pl.when(has_low)
    def _():
        greet(device - 1)

    @pl.when(has_high)
    def _():
        greet(device + 1)

    x_own = nx // SUB
    own_low, own_high = PAD_X // SUB, (PAD_X + nx) // SUB
    blank_low = jnp.zeros((own_low, SUB, LANES), BF16)
    blank_high = jnp.zeros((x_blocks - own_high, SUB, LANES), BF16)

    def margins(ref, at):
        at = at * x_blocks
        ref[pl.ds(at, own_low)] = blank_low
        ref[pl.ds(at + own_high, x_blocks - own_high)] = blank_high

    def all_margins(y, _):
        for g in range(3):
            margins(b_t, g * B_PLANES + B_OFF - HALO + y)
        return 0

    def first_margins(y, _):
        margins(a_t, A_OFF + y)
        return 0

    lax.fori_loop(0, CY + 2 * HALO, all_margins, 0)
    lax.fori_loop(0, CY, first_margins, 0)

    def blank(ref, begin, end):
        def one(y, _):
            ref[pl.ds(y * x_blocks, x_blocks)] = jnp.zeros((x_blocks, SUB, LANES), BF16)
            return 0

        lax.fori_loop(begin, end, one, 0)

    for g in range(3):
        plane = g * B_PLANES + B_OFF + CY
        blank(b_t, plane + jnp.where(no_high, 0, HALO), plane + B_OFF)
    b_t[3 * B_PLANES * x_blocks] = jnp.zeros((SUB, LANES), BF16)

    @pl.when(no_low)
    def _():
        blank(a_t, 0, A_OFF)
        for g in range(3):
            blank(b_t, g * B_PLANES, g * B_PLANES + B_OFF)
        for r in range(win.shape[0]):
            win_low[r] = 0
            for q in range(3):
                sh_low[q, r] = 0

    @pl.when(no_high)
    def _():
        blank(a_t, A_OFF + CY, A_PLANES)
        for r in range(win.shape[0]):
            win_high[r] = 0
            for q in range(3):
                sh_high[q, r] = 0

    pl.semaphore_wait(barrier, has_low.astype(jnp.int32) + has_high.astype(jnp.int32))

    def copy(src, dst, slot, to):
        return pltpu.make_async_remote_copy(
            src_ref=src,
            dst_ref=dst,
            send_sem=send.at[slot],
            recv_sem=recv.at[slot],
            device_id={"span": to},
            device_id_type=pl.DeviceIdType.MESH,
        )

    up = [
        copy(win_hbm, win_low, 0, device + 1),
        copy(sh_hbm, sh_low, 1, device + 1),
        copy(b_hbm.at[pl.ds(CY - HALO, HALO)], low_raw, 2, device + 1),
    ]
    down = [
        copy(win_hbm, win_high, 3, device - 1),
        copy(sh_hbm, sh_high, 4, device - 1),
        copy(b_hbm.at[pl.ds(0, HALO)], high_raw, 5, device - 1),
    ]

    def exchange(up, down):
        @pl.when(has_high)
        def _():
            for c in up:
                c.start()

        @pl.when(has_low)
        def _():
            for c in down:
                c.start()

    def settle(up, down):
        @pl.when(has_high)
        def _():
            for c in up:
                c.wait_send()
            for c in down:
                c.wait_recv()

        @pl.when(has_low)
        def _():
            for c in down:
                c.wait_send()
            for c in up:
                c.wait_recv()

    exchange(up, down)

    tail = jnp.zeros((LANES - nz, nx), BF16)
    def turned(plane):
        return jnp.concatenate([plane, tail], axis=0).T

    def put(ref, at, plane):
        ref[pl.ds(at * x_blocks + own_low, x_own)] = plane.reshape(x_own, SUB, LANES)

    from_z = lax.broadcasted_iota(jnp.int32, (LANES, 2 * LANES), 0)
    to_z = lax.broadcasted_iota(jnp.int32, (LANES, 2 * LANES), 1)
    back = jnp.where(to_z < LANES, -1, 1)
    mover = jnp.where(from_z == ((to_z + back) & (LANES - 1)), 1.0, 0.0).astype(BF16)

    def put_second(at, plane):
        t = turned(plane)
        put(b_t, B_PLANES + at, t)
        moved = jnp.dot(t, mover, preferred_element_type=F32).astype(BF16)
        put(b_t, at, moved[:, :LANES])
        put(b_t, 2 * B_PLANES + at, moved[:, LANES:])

    def second_at(y, x):
        return (B_PLANES + B_OFF + y) * x_blocks + own_low + x

    def level(plane):
        return jnp.sum(plane.astype(F32), keepdims=True) * (1.0 / (nz * nx))

    def add_up(totals, plane, base, sign):
        x = plane.astype(F32) - base
        return [totals[0] + sign * x, totals[1] + sign * (x * x)]

    for c in range(parts):
        loads[2 * c].wait()
        loads[2 * c + 1].wait()
        if c == 0:
            base_a, base_b = level(a_raw[0]), level(b_raw[0])
            for k in range(2):
                sum_a[k, 0] = jnp.zeros((x_own, SUB, LANES), F32)
                sum_b[k, HALO] = jnp.zeros((x_own, SUB, LANES), F32)

        def prepare(i, _):
            y = c * PREP + i * STEP
            group = c * (PREP // STEP) + i
            for k in range(STEP):
                put_second(B_OFF + y + k, b_raw[y + k])
                put(a_t, A_OFF + y + k, turned(a_raw[y + k]))
            for x in range(x_own):
                totals = [sum_b[0, HALO + y, x], sum_b[1, HALO + y, x]]
                for k in range(STEP):
                    totals = add_up(totals, b_t[second_at(y + k, x)], base_b, 1.0)
                    sum_b[0, HALO + y + k + 1, x] = totals[0]
                    sum_b[1, HALO + y + k + 1, x] = totals[1]
                totals = [sum_a[0, group, x], sum_a[1, group, x]]
                for k in range(STEP):
                    totals = add_up(totals, a_t[(A_OFF + y + k) * x_blocks + own_low + x], base_a, 1.0)
                sum_a[0, group + 1, x] = totals[0]
                sum_a[1, group + 1, x] = totals[1]
            return 0

        lax.fori_loop(0, PREP // STEP, prepare, 0)

    for load in own:
        load.wait()
    settle(up[:2], down[:2])

    def choose(wins, shs, lower, slot):
        count = jnp.int32(0)
        got = [jnp.int32(0)] * 4
        for r in range(win.shape[0]):
            node = wins[r]
            row = (node // GZX) % ROWS_TILE
            fits = (row < 2) if lower else (row >= 2)
            here = fits & (count == slot)
            count = count + fits.astype(jnp.int32)
            values = (node, shs[0, r], shs[1, r], shs[2, r])
            got = [jnp.where(here, v, g) for v, g in zip(values, got)]
        return got

    def edge(cond, own, other):
        return [jnp.where(cond, o, v) for o, v in zip(own, other)]

    def task(kind, slot):
        if kind == 0:
            return choose(win, sh, True, slot), 0, CY
        if kind == 1:
            return choose(win, sh, False, slot), 0, CY
        if kind == 2:
            who = edge(no_low, choose(win, sh, True, slot), choose(win_low, sh_low, False, slot))
            return who, jnp.where(no_low, -SPILL, 0), jnp.where(no_low, 0, CY)
        who = edge(no_high, choose(win, sh, False, slot), choose(win_high, sh_high, True, slot))
        return who, jnp.where(no_high, CY, 0), jnp.where(no_high, CY + SPILL, CY)

    def a_at(y, x):
        return (A_OFF + y) * x_blocks + x

    def b_at(y, x):
        return (B_OFF + y) * x_blocks + x

    def place(kind, slot):
        (node, dy, dz, dx), p0, p1 = task(kind, slot)
        yw = STRIDE * (node // GZX - ROWS_TILE * device) + STRIDE // 2 - HALF
        z0 = STRIDE * ((node % GZX) // GX) + STRIDE // 2 - HALF
        xa = STRIDE * (node % GX) + STRIDE // 2 - HALF + PAD_X
        xb = xa + dx - 1
        ya = jnp.maximum(yw, p0)
        yb = jnp.minimum(yw + W, p1)
        ny = jnp.maximum(yb - ya, 0)
        from_start, to_end = ya == yw, yb == yw + W
        xa0, xb0 = xa // SUB, xb // SUB
        off_a, off_b = xa - SUB * xa0, xb - SUB * xb0
        return ya, dy, dz, z0, ny, from_start, to_end, xa0, off_a, xb0, off_b

    def blocks(ref, at):
        return [ref[at + k] for k in range(XR // SUB)]

    row = lax.broadcasted_iota(jnp.int32, (XR, LANES), 0)
    lane = lax.broadcasted_iota(jnp.int32, (XR, LANES), 1)

    def masks(z0, off_a):
        return ((lane - z0) & (LANES - 1)) < W, (row >= off_a) & (row < off_a + W)

    def clip(v, lo, hi):
        return jnp.minimum(jnp.maximum(v, lo), hi)

    def pivot(kind, slot):
        ya, _, _, z0, ny, _, _, xa0, off_a, _, _ = place(kind, slot)
        z_in, x_in = masks(z0, off_a)
        y = clip(ya + ny // 2, 0, CY - 1)
        a = jnp.concatenate(blocks(a_t, a_at(y, xa0)), axis=0).astype(F32)
        pa = jnp.sum(jnp.where(z_in & x_in, a, 0.0), keepdims=True) * (1.0 / (W * W))
        pivots[kind * SLOTS + slot] = jnp.broadcast_to(pa, (SUB, LANES)).astype(BF16)

    for kind in range(4):
        for slot in range(SLOTS):
            pivot(kind, slot)

    settle(up[2:], down[2:])

    @pl.when(has_low)
    def _():
        for k in range(HALO):
            put_second(B_OFF - HALO + k, low_raw[k])
        for x in range(x_own):
            totals = [sum_b[0, HALO, x], sum_b[1, HALO, x]]
            for k in range(HALO):
                plane = b_t[second_at(-1 - k, x)]
                totals = add_up(totals, plane, base_b, -1.0)
                sum_b[0, HALO - 1 - k, x] = totals[0]
                sum_b[1, HALO - 1 - k, x] = totals[1]

    @pl.when(has_high)
    def _():
        for k in range(HALO):
            put_second(B_OFF + CY + k, high_raw[k])
        for x in range(x_own):
            totals = [sum_b[0, HALO + CY, x], sum_b[1, HALO + CY, x]]
            for k in range(HALO):
                plane = b_t[second_at(CY + k, x)]
                totals = add_up(totals, plane, base_b, 1.0)
                sum_b[0, HALO + CY + k + 1, x] = totals[0]
                sum_b[1, HALO + CY + k + 1, x] = totals[1]

    parts_s = (s0, s1, s2, s3)
    row_g = lax.broadcasted_iota(jnp.int32, (XR, 3 * XR), 0)
    col_g = lax.broadcasted_iota(jnp.int32, (XR, 3 * XR), 1) & (XR - 1)

    def tiled(v):
        return jnp.concatenate([v] * (XR // 16), axis=0)

    lane_1 = lax.broadcasted_iota(jnp.int32, (1, LANES), 1)
    row_b = lax.broadcasted_iota(jnp.int32, (XR + SUB, LANES), 0)
    lane_b = lax.broadcasted_iota(jnp.int32, (XR + SUB, LANES), 1)
    b_lo, b_hi = jnp.where(no_low, 0, -HALO), jnp.where(no_high, CY, CY + HALO)

    def part_sums(ref, begin, end, x0, count, keep, base, total, held):
        outside = (total - held).astype(F32)
        got = []
        for k in range(2):
            rows = []
            for b in range(count):
                x = clip(x0 + b - own_low, 0, x_own - 1)
                rows.append(ref[k, end, x] - ref[k, begin, x])
            v = jnp.where(keep, jnp.concatenate(rows, axis=0), 0.0)
            extra = base * base if k else -base
            line = jnp.sum(v, axis=0, keepdims=True)
            got.append(line + jnp.where(lane_1 == 0, extra * outside, 0.0))
        return got

    def wide(line):
        line = line + pltpu.roll(line, XR, 1)
        return jnp.concatenate([line, line[:, :XR]], axis=1)

    def only(value):
        return jnp.where(lane_1 == 0, value, 0.0)

    def correlate(kind, planes, slot):
        a_s = parts_s[kind]
        ya, dy, dz, z0, ny, from_start, to_end, xa0, off_a, xb0, off_b = place(kind, slot)
        at = kind * SLOTS + slot
        z_in, x_in = masks(z0, off_a)
        zero = jnp.zeros((XR, LANES), BF16)
        keep_a = jnp.where(z_in & x_in, 1.0, 0.0).astype(BF16)
        ones_a = jnp.where(z_in & (row == XR - 1), 1.0, 0.0).astype(BF16)
        wrap = jnp.where(row[:16] < off_b, 1.0, 0.0).astype(BF16)
        stay = jnp.where(row[:16] < off_b, 0.0, 1.0).astype(BF16)
        pa = tiled(pivots[at])
        turn = dz & (LANES - 1)
        start_a = a_at(ya, xa0)
        for k in (0, 1, planes + 2, planes + 3):
            a_s[k] = zero

        def first(t):
            raw = jnp.concatenate(blocks(a_t, start_a + t * x_blocks), axis=0)
            valid = t < ny
            v = (raw - pa) * keep_a + ones_a
            if planes < LEAST or t >= LEAST:
                v = jnp.where(valid, v, zero)
            a_s[t + 2] = pltpu.roll(v, turn, 1)

        some = ny > 0
        start_b = b_at(ya + dy - 1, xb0)
        first_x, first_b = SUB * xa0 - PAD_X, SUB * xb0 - PAD_X
        y0, y1 = clip(ya, 0, CY), clip(ya + ny, 0, CY)
        rows_in = clip(first_x + off_a + W, 0, nx) - clip(first_x + off_a, 0, nx)
        n_a = ny * (W * W)
        stats = part_sums(
            sum_a, y0 // STEP, y1 // STEP, xa0, XR // SUB,
            z_in & x_in & (row + first_x >= 0) & (row + first_x < nx),
            base_a, n_a, (y1 - y0) * rows_in * W,
        )
        v0 = ya + dy - jnp.where(from_start, 1, 0)
        v1 = ya + dy + ny + jnp.where(to_end, 1, 0)
        v1 = jnp.where(some, v1, v0)
        n_b = (v1 - v0) * (BW * BW)
        v0, v1 = clip(v0, b_lo, b_hi), clip(v1, b_lo, b_hi)
        rows_in = clip(first_b + off_b + BW, 0, nx) - clip(first_b + off_b, 0, nx)
        stats += part_sums(
            sum_b, HALO + v0, HALO + v1, xb0, XR // SUB + 1,
            (((lane_b - z0 - dz + 1) & (LANES - 1)) < BW)
            & (row_b >= off_b) & (row_b < off_b + BW)
            & (row_b + first_b >= 0) & (row_b + first_b < nx),
            base_b, n_b, (v1 - v0) * rows_in * BW,
        )
        stats += [
            only(pivots[at, 0:1, 0:1].astype(F32)),
            only(n_a.astype(F32)),
            only(n_b.astype(F32)),
            only(base_a),
            only(base_b),
        ]
        for k, line in enumerate(stats):
            lines[18 + k, pl.ds(at, 1), :] = wide(line)

        def second(u):
            got = []
            for g in range(3):
                at_b = start_b + (g * B_PLANES + u) * x_blocks
                t = blocks(b_t, at_b)
                t[0] = t[0] * stay + b_t[at_b + XR // SUB] * wrap
                got.extend(t)
            return jnp.concatenate(got, axis=0)

        gram = jnp.zeros((3 * XR, 3 * XR), F32)
        done = 0
        begin = 0
        for size in sizes(planes):
            for t in range(done, min(begin + size, planes)):
                first(t)
            done = min(begin + size, planes)
            us = range(begin, begin + size)
            left = jnp.concatenate(
                [jnp.concatenate([a_s[u - f + 2] for u in us], axis=1) for f in range(3)], axis=0
            )
            right = jnp.concatenate([second(u) for u in us], axis=1)
            gram = gram + lax.dot_general(
                left, right, (((1,), (1,)), ((), ())), preferred_element_type=F32
            )
            begin += size

        gap = (col_g - row_g - (off_b - off_a)) & (XR - 1)
        real = row_g < XR - 1
        picks = [real & (gap == e) for e in range(3)]
        out_lines = []
        for f in range(3):
            block = gram[f * XR : (f + 1) * XR, :]
            for e in range(3):
                out_lines.append(jnp.sum(jnp.where(picks[e], block, 0.0), axis=0, keepdims=True))
        t_col = (col_g[:1] - off_b) & (XR - 1)
        for f in range(3):
            line = gram[(f + 1) * XR - 1 : (f + 1) * XR, :]
            for e in range(3):
                out_lines.append(jnp.where((t_col >= e) & (t_col < e + W), line, 0.0))
        for q, line in enumerate(out_lines):
            lines[q, pl.ds(at, 1), :] = line

    def every_kind(slot, _):
        for kind, planes in enumerate(PLANES):
            correlate(kind, planes, slot)
        return 0

    lax.fori_loop(0, SLOTS, every_kind, 0)

    seg = lax.broadcasted_iota(jnp.int32, (8, 3 * XR), 0)
    seg_lane = lax.broadcasted_iota(jnp.int32, (8, 3 * XR), 1)
    select = jnp.where(seg_lane // XR == seg, 1.0, 0.0)
    table = lax.dot_general(
        select,
        lines[...].reshape(LINES * TASKS, 3 * XR),
        (((1,), (1,)), ((), ())),
        precision=lax.Precision.HIGHEST,
        preferred_element_type=F32,
    )
    table = jnp.concatenate([table, jnp.zeros((8, 4 * LANES - LINES * TASKS), F32)], axis=1)
    mine[...] = table

    def turn_lanes(v, by):
        pieces = [v[:, k * LANES : (k + 1) * LANES] for k in range(4)]
        return jnp.concatenate([pltpu.roll(p, by, 1) for p in pieces], axis=1)

    up = [copy(mine, low, 6, device + 1)]
    down = [copy(mine, high, 7, device - 1)]
    exchange(up, down)

    @pl.when(no_low)
    def _():
        low[...] = turn_lanes(mine[...], 4)

    @pl.when(no_high)
    def _():
        high[...] = turn_lanes(mine[...], LANES - 4)

    settle(up, down)

    lower, upper = low[...], high[...]
    task_lane = lax.broadcasted_iota(jnp.int32, (8, 4 * LANES), 1) & (TASKS - 1)
    other = jnp.where(
        task_lane < 4,
        turn_lanes(lower, LANES - 12),
        jnp.where(
            task_lane < 8,
            turn_lanes(upper, LANES - 4),
            jnp.where(task_lane < 12, turn_lanes(lower, 4), turn_lanes(upper, 12)),
        ),
    )

    def spread(v):
        got = []
        for q in range(LINES):
            piece = v[:, q // 8 * LANES : (q // 8 + 1) * LANES]
            by = (LANES - TASKS * (q % 8)) % LANES
            got.append(pltpu.roll(piece, by, 1) if by else piece)
        return got

    both = [spread(mine[...]), spread(other)]
    mean_a = sum(p[18] + p[23] * p[25] for p in both) / float(W) ** 3
    mean_b = sum(p[20] + p[24] * p[26] for p in both) / float(BW) ** 3
    energy_a = jnp.zeros((8, LANES), F32)
    energy_b = jnp.zeros((8, LANES), F32)
    corr = [jnp.zeros((8, LANES), F32)] * 9
    for p in both:
        da, db = p[25] - mean_a, p[26] - mean_b
        energy_a += p[19] + 2.0 * da * p[18] + p[23] * da * da
        energy_b += p[21] + 2.0 * db * p[20] + p[24] * db * db
        rest = -mean_b * (p[18] + p[23] * da)
        da = p[22] - mean_a
        corr = [v + (p[q] + da * p[9 + q] + rest) for q, v in enumerate(corr)]
    energy_a = energy_a / float(W) ** 3
    energy_b = energy_b / float(BW) ** 3
    normaliser = float(W) ** 3 * jnp.sqrt((energy_a + EPSILON) * (energy_b + EPSILON))
    row_s = lax.broadcasted_iota(jnp.int32, (8, LANES), 0)
    weights = [jnp.where(row_s < 3, jnp.exp(SHARP * (c / normaliser)), 0.0) for c in corr]
    by_z = sum(weights)
    by_y = sum(weights[6:]) - sum(weights[:3])
    by_x = sum(weights[2::3]) - sum(weights[0::3])
    total = jnp.sum(by_z, axis=0, keepdims=True)
    along = (
        jnp.sum(by_y, axis=0, keepdims=True) / total,
        (by_z[2:3] - by_z[0:1]) / total,
        jnp.sum(by_x, axis=0, keepdims=True) / total,
    )
    row_f = lax.broadcasted_iota(jnp.int32, (8, GZX), 0)
    lane_f = lax.broadcasted_iota(jnp.int32, (8, GZX), 1)
    fields = [jnp.zeros((8, GZX), F32) for _ in range(3)]
    for kind in range(4):
        for slot in range(SLOTS):
            at = kind * SLOTS + slot
            node = task(kind, slot)[0][0]
            at_row = node // GZX - ROWS_TILE * device + 1
            if kind == 2:
                at_row = jnp.where(no_low, -1, at_row)
            if kind == 3:
                at_row = jnp.where(no_high, -1, at_row)
            hit = (row_f == at_row) & (lane_f == node % GZX)
            for c in range(3):
                fields[c] = jnp.where(hit, along[c][:, at : at + 1], fields[c])
    deep = lane_f // GX
    stream = lane_f % GX
    for c in range(3):
        u = fields[c]
        near = (
            jnp.where(deep < GZ - 1, pltpu.roll(u, GZX - GX, 1), 0.0)
            + jnp.where(deep > 0, pltpu.roll(u, GX, 1), 0.0)
            + jnp.where(stream < GX - 1, pltpu.roll(u, GZX - 1, 1), 0.0)
            + jnp.where(stream > 0, pltpu.roll(u, 1, 1), 0.0)
        )
        near = near + pltpu.roll(u, 7, 0) + pltpu.roll(u, 1, 0)
        smooth = 0.4 * u + 0.1 * near
        out[c] = smooth[1 : 1 + ROWS_TILE]


def shards(first_exposure, second_exposure, windows, shifts):
    n = lax.axis_size("span")
    nz, nx = first_exposure.shape[1:]
    x_blocks = (PAD_X + nx + PAD_X) // SUB
    hbm = pl.BlockSpec(memory_space=pltpu.HBM)
    return pl.pallas_call(
        functools.partial(kernel, n),
        name="update",
        out_shape=jax.ShapeDtypeStruct((3, CY // STRIDE, GZX), F32),
        in_specs=[hbm] * 4,
        out_specs=pl.BlockSpec(memory_space=pltpu.VMEM),
        scratch_shapes=[
            pltpu.SMEM(windows.shape, jnp.int32),
            pltpu.SMEM(shifts.shape, jnp.int32),
            pltpu.VMEM((CY, nz, nx), BF16),
            pltpu.VMEM((CY, nz, nx), BF16),
            pltpu.VMEM((HALO, nz, nx), BF16),
            pltpu.VMEM((HALO, nz, nx), BF16),
            pltpu.SMEM(windows.shape, jnp.int32),
            pltpu.SMEM(windows.shape, jnp.int32),
            pltpu.SMEM(shifts.shape, jnp.int32),
            pltpu.SMEM(shifts.shape, jnp.int32),
            pltpu.VMEM((A_PLANES * x_blocks, SUB, LANES), BF16),
            pltpu.VMEM((3 * B_PLANES * x_blocks + 1, SUB, LANES), BF16),
            *(pltpu.VMEM((p + 4, XR, LANES), BF16) for p in PLANES),
            pltpu.VMEM((TASKS, SUB, LANES), BF16),
            pltpu.VMEM((2, CY // STEP + 1, nx // SUB, SUB, LANES), F32),
            pltpu.VMEM((2, CY + 2 * HALO + 1, nx // SUB, SUB, LANES), F32),
            pltpu.VMEM((LINES, TASKS, 3 * XR), F32),
            pltpu.VMEM((8, 4 * LANES), F32),
            pltpu.VMEM((8, 4 * LANES), F32),
            pltpu.VMEM((8, 4 * LANES), F32),
            pltpu.SemaphoreType.DMA((8,)),
            pltpu.SemaphoreType.DMA((8,)),
            pltpu.SemaphoreType.DMA((2 * (CY // PREP) + 2,)),
        ],
        compiler_params=pltpu.CompilerParams(
            collective_id=0, has_side_effects=True, vmem_limit_bytes=VMEM_BYTES
        ),
    )(windows, shifts, first_exposure, second_exposure)


def solution(mesh):
    in_specs = (
        P(("grp", "span"), None, None),
        P(("grp", "span"), None, None),
        P(("grp", "span")),
        P(None, ("grp", "span")),
    )
    out_specs = P(None, ("grp", "span"), None)
    return jax.shard_map(shards, mesh=mesh, in_specs=in_specs, out_specs=out_specs, check_vma=False)
```

```python
import functools

import jax
import jax.numpy as jnp
from jax import lax
from jax.experimental import pallas as pl
from jax.experimental.pallas import tpu as pltpu
from jax.sharding import PartitionSpec as P

W = 48
STRIDE = 12
DYM = 3
GZ = 8
GX = 16
GZX = 128
HALO = DYM + 1
HALF = W // 2
BW = W + 2
ROWS_TILE = 5
CY = STRIDE * ROWS_TILE
SPILL = 18
LOWER = 42
LEAST = 30
SLOTS = 4
TASKS = 16

SHARP = 80.0
EPSILON = 1e-06

F32 = jnp.float32
BF16 = jnp.bfloat16

PAD_X = 32
XR = 64
LANES = 128
SUB = 16
A_OFF = SPILL
A_PLANES = SPILL + CY + SPILL
B_OFF = SPILL + HALO
B_PLANES = B_OFF + CY + B_OFF
CHUNK = 10
PLANES = (LOWER, W, SPILL, SPILL)
VMEM_BYTES = 62 << 20
PREP = 12
STEP = 6
LINES = 27


def sizes(n):
    total = n + 2
    out = []
    while total > 0:
        out.append(min(CHUNK, total))
        total -= CHUNK
    return out


def kernel(
    n, win_hbm, sh_hbm, a_hbm, b_hbm, out,
    win, sh, a_raw, b_raw, low_raw, high_raw, win_low, win_high, sh_low, sh_high,
    a_t, b_t, s0, s1, s2, s3, pivots, sum_a, sum_b, lines, mine, low, high, send, recv, sems,
):
    nz, nx = a_hbm.shape[1], a_hbm.shape[2]
    x_blocks = (PAD_X + nx + PAD_X) // SUB
    device = lax.axis_index("span")
    last = n - 1
    has_low, has_high = device > 0, device < last
    no_low, no_high = device == 0, device == last
    parts = CY // PREP
    loads = []
    for c in range(parts):
        rows = pl.ds(c * PREP, PREP)
        loads.append(pltpu.make_async_copy(b_hbm.at[rows], b_raw.at[rows], sems.at[2 * c]))
        loads.append(pltpu.make_async_copy(a_hbm.at[rows], a_raw.at[rows], sems.at[2 * c + 1]))
    own = [
        pltpu.make_async_copy(win_hbm, win, sems.at[2 * parts]),
        pltpu.make_async_copy(sh_hbm, sh, sems.at[2 * parts + 1]),
    ]
    for load in own + loads:
        load.start()

    barrier = pltpu.get_barrier_semaphore()

    def greet(to):
        pl.semaphore_signal(
            barrier, inc=1, device_id={"span": to}, device_id_type=pl.DeviceIdType.MESH
        )

    @pl.when(has_low)
    def _():
        greet(device - 1)

    @pl.when(has_high)
    def _():
        greet(device + 1)

    x_own = nx // SUB
    own_low, own_high = PAD_X // SUB, (PAD_X + nx) // SUB
    blank_low = jnp.zeros((own_low, SUB, LANES), BF16)
    blank_high = jnp.zeros((x_blocks - own_high, SUB, LANES), BF16)

    def margins(ref, at):
        at = at * x_blocks
        ref[pl.ds(at, own_low)] = blank_low
        ref[pl.ds(at + own_high, x_blocks - own_high)] = blank_high

    def all_margins(y, _):
        for g in range(3):
            margins(b_t, g * B_PLANES + B_OFF - HALO + y)
        return 0

    def first_margins(y, _):
        margins(a_t, A_OFF + y)
        return 0

    lax.fori_loop(0, CY + 2 * HALO, all_margins, 0)
    lax.fori_loop(0, CY, first_margins, 0)

    def blank(ref, begin, end):
        def one(y, _):
            ref[pl.ds(y * x_blocks, x_blocks)] = jnp.zeros((x_blocks, SUB, LANES), BF16)
            return 0

        lax.fori_loop(begin, end, one, 0)

    for g in range(3):
        plane = g * B_PLANES + B_OFF + CY
        blank(b_t, plane + jnp.where(no_high, 0, HALO), plane + B_OFF)
    b_t[3 * B_PLANES * x_blocks] = jnp.zeros((SUB, LANES), BF16)

    @pl.when(no_low)
    def _():
        blank(a_t, 0, A_OFF)
        for g in range(3):
            blank(b_t, g * B_PLANES, g * B_PLANES + B_OFF)
        for r in range(win.shape[0]):
            win_low[r] = 0
            for q in range(3):
                sh_low[q, r] = 0

    @pl.when(no_high)
    def _():
        blank(a_t, A_OFF + CY, A_PLANES)
        for r in range(win.shape[0]):
            win_high[r] = 0
            for q in range(3):
                sh_high[q, r] = 0


    def copy(src, dst, slot, to):
        return pltpu.make_async_remote_copy(
            src_ref=src,
            dst_ref=dst,
            send_sem=send.at[slot],
            recv_sem=recv.at[slot],
            device_id={"span": to},
            device_id_type=pl.DeviceIdType.MESH,
        )

    up = [
        copy(win_hbm, win_low, 0, device + 1),
        copy(sh_hbm, sh_low, 1, device + 1),
        copy(b_hbm.at[pl.ds(CY - HALO, HALO)], low_raw, 2, device + 1),
    ]
    down = [
        copy(win_hbm, win_high, 3, device - 1),
        copy(sh_hbm, sh_high, 4, device - 1),
        copy(b_hbm.at[pl.ds(0, HALO)], high_raw, 5, device - 1),
    ]

    def exchange(up, down):
        @pl.when(has_high)
        def _():
            for c in up:
                c.start()

        @pl.when(has_low)
        def _():
            for c in down:
                c.start()

    def settle(up, down):
        @pl.when(has_high)
        def _():
            for c in up:
                c.wait_send()
            for c in down:
                c.wait_recv()

        @pl.when(has_low)
        def _():
            for c in down:
                c.wait_send()
            for c in up:
                c.wait_recv()

    tail = jnp.zeros((LANES - nz, nx), BF16)
    def turned(plane):
        return jnp.concatenate([plane, tail], axis=0).T

    def put(ref, at, plane):
        ref[pl.ds(at * x_blocks + own_low, x_own)] = plane.reshape(x_own, SUB, LANES)

    from_z = lax.broadcasted_iota(jnp.int32, (LANES, 2 * LANES), 0)
    to_z = lax.broadcasted_iota(jnp.int32, (LANES, 2 * LANES), 1)
    back = jnp.where(to_z < LANES, -1, 1)
    mover = jnp.where(from_z == ((to_z + back) & (LANES - 1)), 1.0, 0.0).astype(BF16)

    def put_second(at, plane):
        t = turned(plane)
        put(b_t, B_PLANES + at, t)
        moved = jnp.dot(t, mover, preferred_element_type=F32).astype(BF16)
        put(b_t, at, moved[:, :LANES])
        put(b_t, 2 * B_PLANES + at, moved[:, LANES:])

    def second_at(y, x):
        return (B_PLANES + B_OFF + y) * x_blocks + own_low + x

    def level(plane):
        return jnp.sum(plane.astype(F32), keepdims=True) * (1.0 / (nz * nx))

    def add_up(totals, plane, base, sign):
        x = plane.astype(F32) - base
        return [totals[0] + sign * x, totals[1] + sign * (x * x)]

    for c in range(parts):
        if c == 1:
            pl.semaphore_wait(barrier, has_low.astype(jnp.int32) + has_high.astype(jnp.int32))
            exchange(up, down)
        loads[2 * c].wait()
        loads[2 * c + 1].wait()
        if c == 0:
            base_a, base_b = level(a_raw[0]), level(b_raw[0])
            for k in range(2):
                sum_a[k, 0] = jnp.zeros((x_own, SUB, LANES), F32)
                sum_b[k, HALO] = jnp.zeros((x_own, SUB, LANES), F32)

        def prepare(i, _):
            y = c * PREP + i * STEP
            group = c * (PREP // STEP) + i
            for k in range(STEP):
                put_second(B_OFF + y + k, b_raw[y + k])
                put(a_t, A_OFF + y + k, turned(a_raw[y + k]))
            for x in range(x_own):
                totals = [sum_b[0, HALO + y, x], sum_b[1, HALO + y, x]]
                for k in range(STEP):
                    totals = add_up(totals, b_t[second_at(y + k, x)], base_b, 1.0)
                    sum_b[0, HALO + y + k + 1, x] = totals[0]
                    sum_b[1, HALO + y + k + 1, x] = totals[1]
                totals = [sum_a[0, group, x], sum_a[1, group, x]]
                for k in range(STEP):
                    totals = add_up(totals, a_t[(A_OFF + y + k) * x_blocks + own_low + x], base_a, 1.0)
                sum_a[0, group + 1, x] = totals[0]
                sum_a[1, group + 1, x] = totals[1]
            return 0

        lax.fori_loop(0, PREP // STEP, prepare, 0)

    for load in own:
        load.wait()
    settle(up[:2], down[:2])

    def choose(wins, shs, lower, slot):
        count = jnp.int32(0)
        got = [jnp.int32(0)] * 4
        for r in range(win.shape[0]):
            node = wins[r]
            row = (node // GZX) % ROWS_TILE
            fits = (row < 2) if lower else (row >= 2)
            here = fits & (count == slot)
            count = count + fits.astype(jnp.int32)
            values = (node, shs[0, r], shs[1, r], shs[2, r])
            got = [jnp.where(here, v, g) for v, g in zip(values, got)]
        return got

    def edge(cond, own, other):
        return [jnp.where(cond, o, v) for o, v in zip(own, other)]

    def task(kind, slot):
        if kind == 0:
            return choose(win, sh, True, slot), 0, CY
        if kind == 1:
            return choose(win, sh, False, slot), 0, CY
        if kind == 2:
            who = edge(no_low, choose(win, sh, True, slot), choose(win_low, sh_low, False, slot))
            return who, jnp.where(no_low, -SPILL, 0), jnp.where(no_low, 0, CY)
        who = edge(no_high, choose(win, sh, False, slot), choose(win_high, sh_high, True, slot))
        return who, jnp.where(no_high, CY, 0), jnp.where(no_high, CY + SPILL, CY)

    def a_at(y, x):
        return (A_OFF + y) * x_blocks + x

    def b_at(y, x):
        return (B_OFF + y) * x_blocks + x

    def place(kind, slot):
        (node, dy, dz, dx), p0, p1 = task(kind, slot)
        yw = STRIDE * (node // GZX - ROWS_TILE * device) + STRIDE // 2 - HALF
        z0 = STRIDE * ((node % GZX) // GX) + STRIDE // 2 - HALF
        xa = STRIDE * (node % GX) + STRIDE // 2 - HALF + PAD_X
        xb = xa + dx - 1
        ya = jnp.maximum(yw, p0)
        yb = jnp.minimum(yw + W, p1)
        ny = jnp.maximum(yb - ya, 0)
        from_start, to_end = ya == yw, yb == yw + W
        xa0, xb0 = xa // SUB, xb // SUB
        off_a, off_b = xa - SUB * xa0, xb - SUB * xb0
        return ya, dy, dz, z0, ny, from_start, to_end, xa0, off_a, xb0, off_b

    def blocks(ref, at):
        return [ref[at + k] for k in range(XR // SUB)]

    row = lax.broadcasted_iota(jnp.int32, (XR, LANES), 0)
    lane = lax.broadcasted_iota(jnp.int32, (XR, LANES), 1)

    def masks(z0, off_a):
        return ((lane - z0) & (LANES - 1)) < W, (row >= off_a) & (row < off_a + W)

    def clip(v, lo, hi):
        return jnp.minimum(jnp.maximum(v, lo), hi)

    def pivot(kind, slot):
        ya, _, _, z0, ny, _, _, xa0, off_a, _, _ = place(kind, slot)
        z_in, x_in = masks(z0, off_a)
        y = clip(ya + ny // 2, 0, CY - 1)
        a = jnp.concatenate(blocks(a_t, a_at(y, xa0)), axis=0).astype(F32)
        pa = jnp.sum(jnp.where(z_in & x_in, a, 0.0), keepdims=True) * (1.0 / (W * W))
        pivots[kind * SLOTS + slot] = jnp.broadcast_to(pa, (SUB, LANES)).astype(BF16)

    for kind in range(4):
        for slot in range(SLOTS):
            pivot(kind, slot)

    settle(up[2:], down[2:])

    @pl.when(has_low)
    def _():
        for k in range(HALO):
            put_second(B_OFF - HALO + k, low_raw[k])
        for x in range(x_own):
            totals = [sum_b[0, HALO, x], sum_b[1, HALO, x]]
            for k in range(HALO):
                plane = b_t[second_at(-1 - k, x)]
                totals = add_up(totals, plane, base_b, -1.0)
                sum_b[0, HALO - 1 - k, x] = totals[0]
                sum_b[1, HALO - 1 - k, x] = totals[1]

    @pl.when(has_high)
    def _():
        for k in range(HALO):
            put_second(B_OFF + CY + k, high_raw[k])
        for x in range(x_own):
            totals = [sum_b[0, HALO + CY, x], sum_b[1, HALO + CY, x]]
            for k in range(HALO):
                plane = b_t[second_at(CY + k, x)]
                totals = add_up(totals, plane, base_b, 1.0)
                sum_b[0, HALO + CY + k + 1, x] = totals[0]
                sum_b[1, HALO + CY + k + 1, x] = totals[1]

    parts_s = (s0, s1, s2, s3)
    row_g = lax.broadcasted_iota(jnp.int32, (XR, 3 * XR), 0)
    col_g = lax.broadcasted_iota(jnp.int32, (XR, 3 * XR), 1) & (XR - 1)

    def tiled(v):
        return jnp.concatenate([v] * (XR // 16), axis=0)

    lane_1 = lax.broadcasted_iota(jnp.int32, (1, LANES), 1)
    row_b = lax.broadcasted_iota(jnp.int32, (XR + SUB, LANES), 0)
    lane_b = lax.broadcasted_iota(jnp.int32, (XR + SUB, LANES), 1)
    b_lo, b_hi = jnp.where(no_low, 0, -HALO), jnp.where(no_high, CY, CY + HALO)

    def part_sums(ref, begin, end, x0, count, keep, base, total, held):
        outside = (total - held).astype(F32)
        got = []
        for k in range(2):
            rows = []
            for b in range(count):
                x = clip(x0 + b - own_low, 0, x_own - 1)
                rows.append(ref[k, end, x] - ref[k, begin, x])
            v = jnp.where(keep, jnp.concatenate(rows, axis=0), 0.0)
            extra = base * base if k else -base
            line = jnp.sum(v, axis=0, keepdims=True)
            got.append(line + jnp.where(lane_1 == 0, extra * outside, 0.0))
        return got

    def wide(line):
        line = line + pltpu.roll(line, XR, 1)
        return jnp.concatenate([line, line[:, :XR]], axis=1)

    def only(value):
        return jnp.where(lane_1 == 0, value, 0.0)

    def correlate(kind, planes, slot):
        a_s = parts_s[kind]
        ya, dy, dz, z0, ny, from_start, to_end, xa0, off_a, xb0, off_b = place(kind, slot)
        at = kind * SLOTS + slot
        z_in, x_in = masks(z0, off_a)
        zero = jnp.zeros((XR, LANES), BF16)
        keep_a = jnp.where(z_in & x_in, 1.0, 0.0).astype(BF16)
        ones_a = jnp.where(z_in & (row == XR - 1), 1.0, 0.0).astype(BF16)
        wrap = jnp.where(row[:16] < off_b, 1.0, 0.0).astype(BF16)
        pa = tiled(pivots[at])
        turn = dz & (LANES - 1)
        start_a = a_at(ya, xa0)
        for k in (0, 1, planes + 2, planes + 3):
            a_s[k] = zero

        def first(t):
            raw = jnp.concatenate(blocks(a_t, start_a + t * x_blocks), axis=0)
            valid = t < ny
            v = (raw - pa) * keep_a + ones_a
            if planes < LEAST or t >= LEAST:
                v = jnp.where(valid, v, zero)
            a_s[t + 2] = pltpu.roll(v, turn, 1)

        some = ny > 0
        start_b = b_at(ya + dy - 1, xb0)
        first_x, first_b = SUB * xa0 - PAD_X, SUB * xb0 - PAD_X
        y0, y1 = clip(ya, 0, CY), clip(ya + ny, 0, CY)
        rows_in = clip(first_x + off_a + W, 0, nx) - clip(first_x + off_a, 0, nx)
        n_a = ny * (W * W)
        stats = part_sums(
            sum_a, y0 // STEP, y1 // STEP, xa0, XR // SUB,
            z_in & x_in & (row + first_x >= 0) & (row + first_x < nx),
            base_a, n_a, (y1 - y0) * rows_in * W,
        )
        v0 = ya + dy - jnp.where(from_start, 1, 0)
        v1 = ya + dy + ny + jnp.where(to_end, 1, 0)
        v1 = jnp.where(some, v1, v0)
        n_b = (v1 - v0) * (BW * BW)
        v0, v1 = clip(v0, b_lo, b_hi), clip(v1, b_lo, b_hi)
        rows_in = clip(first_b + off_b + BW, 0, nx) - clip(first_b + off_b, 0, nx)
        stats += part_sums(
            sum_b, HALO + v0, HALO + v1, xb0, XR // SUB + 1,
            (((lane_b - z0 - dz + 1) & (LANES - 1)) < BW)
            & (row_b >= off_b) & (row_b < off_b + BW)
            & (row_b + first_b >= 0) & (row_b + first_b < nx),
            base_b, n_b, (v1 - v0) * rows_in * BW,
        )
        stats += [
            only(pivots[at, 0:1, 0:1].astype(F32)),
            only(n_a.astype(F32)),
            only(n_b.astype(F32)),
            only(base_a),
            only(base_b),
        ]
        for k, line in enumerate(stats):
            lines[18 + k, pl.ds(at, 1), :] = wide(line)

        def second(u):
            got = []
            for g in range(3):
                at_b = start_b + (g * B_PLANES + u) * x_blocks
                t = blocks(b_t, at_b)
                t[0] = jnp.where(wrap > 0.5, b_t[at_b + XR // SUB], t[0])
                got.extend(t)
            return jnp.concatenate(got, axis=0)

        gram = jnp.zeros((3 * XR, 3 * XR), F32)
        done = 0
        begin = 0
        for size in sizes(planes):
            for t in range(done, min(begin + size, planes)):
                first(t)
            done = min(begin + size, planes)
            us = range(begin, begin + size)
            left = jnp.concatenate(
                [jnp.concatenate([a_s[u - f + 2] for u in us], axis=1) for f in range(3)], axis=0
            )
            right = jnp.concatenate([second(u) for u in us], axis=1)
            gram = gram + lax.dot_general(
                left, right, (((1,), (1,)), ((), ())), preferred_element_type=F32
            )
            begin += size

        gap = (col_g - row_g - (off_b - off_a)) & (XR - 1)
        real = row_g < XR - 1
        picks = [real & (gap == e) for e in range(3)]
        out_lines = []
        for f in range(3):
            block = gram[f * XR : (f + 1) * XR, :]
            for e in range(3):
                out_lines.append(jnp.sum(jnp.where(picks[e], block, 0.0), axis=0, keepdims=True))
        t_col = (col_g[:1] - off_b) & (XR - 1)
        for f in range(3):
            line = gram[(f + 1) * XR - 1 : (f + 1) * XR, :]
            for e in range(3):
                out_lines.append(jnp.where((t_col >= e) & (t_col < e + W), line, 0.0))
        for q, line in enumerate(out_lines):
            lines[q, pl.ds(at, 1), :] = line

    def every_kind(slot, _):
        for kind, planes in enumerate(PLANES):
            correlate(kind, planes, slot)
        return 0

    lax.fori_loop(0, SLOTS, every_kind, 0)

    seg = lax.broadcasted_iota(jnp.int32, (8, 3 * XR), 0)
    seg_lane = lax.broadcasted_iota(jnp.int32, (8, 3 * XR), 1)
    select = jnp.where(seg_lane // XR == seg, 1.0, 0.0)
    table = lax.dot_general(
        select,
        lines[...].reshape(LINES * TASKS, 3 * XR),
        (((1,), (1,)), ((), ())),
        precision=lax.Precision.HIGHEST,
        preferred_element_type=F32,
    )
    table = jnp.concatenate([table, jnp.zeros((8, 4 * LANES - LINES * TASKS), F32)], axis=1)
    mine[...] = table

    def turn_lanes(v, by):
        pieces = [v[:, k * LANES : (k + 1) * LANES] for k in range(4)]
        return jnp.concatenate([pltpu.roll(p, by, 1) for p in pieces], axis=1)

    up = [copy(mine, low, 6, device + 1)]
    down = [copy(mine, high, 7, device - 1)]
    exchange(up, down)

    @pl.when(no_low)
    def _():
        low[...] = turn_lanes(mine[...], 4)

    @pl.when(no_high)
    def _():
        high[...] = turn_lanes(mine[...], LANES - 4)

    settle(up, down)

    lower, upper = low[...], high[...]
    task_lane = lax.broadcasted_iota(jnp.int32, (8, 4 * LANES), 1) & (TASKS - 1)
    other = jnp.where(
        task_lane < 4,
        turn_lanes(lower, LANES - 12),
        jnp.where(
            task_lane < 8,
            turn_lanes(upper, LANES - 4),
            jnp.where(task_lane < 12, turn_lanes(lower, 4), turn_lanes(upper, 12)),
        ),
    )

    def spread(v):
        got = []
        for q in range(LINES):
            piece = v[:, q // 8 * LANES : (q // 8 + 1) * LANES]
            by = (LANES - TASKS * (q % 8)) % LANES
            got.append(pltpu.roll(piece, by, 1) if by else piece)
        return got

    both = [spread(mine[...]), spread(other)]
    mean_a = sum(p[18] + p[23] * p[25] for p in both) / float(W) ** 3
    mean_b = sum(p[20] + p[24] * p[26] for p in both) / float(BW) ** 3
    energy_a = jnp.zeros((8, LANES), F32)
    energy_b = jnp.zeros((8, LANES), F32)
    corr = [jnp.zeros((8, LANES), F32)] * 9
    for p in both:
        da, db = p[25] - mean_a, p[26] - mean_b
        energy_a += p[19] + 2.0 * da * p[18] + p[23] * da * da
        energy_b += p[21] + 2.0 * db * p[20] + p[24] * db * db
        rest = -mean_b * (p[18] + p[23] * da)
        da = p[22] - mean_a
        corr = [v + (p[q] + da * p[9 + q] + rest) for q, v in enumerate(corr)]
    energy_a = energy_a / float(W) ** 3
    energy_b = energy_b / float(BW) ** 3
    normaliser = float(W) ** 3 * jnp.sqrt((energy_a + EPSILON) * (energy_b + EPSILON))
    row_s = lax.broadcasted_iota(jnp.int32, (8, LANES), 0)
    weights = [jnp.where(row_s < 3, jnp.exp(SHARP * (c / normaliser)), 0.0) for c in corr]
    by_z = sum(weights)
    by_y = sum(weights[6:]) - sum(weights[:3])
    by_x = sum(weights[2::3]) - sum(weights[0::3])
    total = jnp.sum(by_z, axis=0, keepdims=True)
    along = (
        jnp.sum(by_y, axis=0, keepdims=True) / total,
        (by_z[2:3] - by_z[0:1]) / total,
        jnp.sum(by_x, axis=0, keepdims=True) / total,
    )
    row_f = lax.broadcasted_iota(jnp.int32, (8, GZX), 0)
    lane_f = lax.broadcasted_iota(jnp.int32, (8, GZX), 1)
    fields = [jnp.zeros((8, GZX), F32) for _ in range(3)]
    for kind in range(4):
        for slot in range(SLOTS):
            at = kind * SLOTS + slot
            node = task(kind, slot)[0][0]
            at_row = node // GZX - ROWS_TILE * device + 1
            if kind == 2:
                at_row = jnp.where(no_low, -1, at_row)
            if kind == 3:
                at_row = jnp.where(no_high, -1, at_row)
            hit = (row_f == at_row) & (lane_f == node % GZX)
            for c in range(3):
                fields[c] = jnp.where(hit, along[c][:, at : at + 1], fields[c])
    deep = lane_f // GX
    stream = lane_f % GX
    for c in range(3):
        u = fields[c]
        near = (
            jnp.where(deep < GZ - 1, pltpu.roll(u, GZX - GX, 1), 0.0)
            + jnp.where(deep > 0, pltpu.roll(u, GX, 1), 0.0)
            + jnp.where(stream < GX - 1, pltpu.roll(u, GZX - 1, 1), 0.0)
            + jnp.where(stream > 0, pltpu.roll(u, 1, 1), 0.0)
        )
        near = near + pltpu.roll(u, 7, 0) + pltpu.roll(u, 1, 0)
        smooth = 0.4 * u + 0.1 * near
        out[c] = smooth[1 : 1 + ROWS_TILE]


def shards(first_exposure, second_exposure, windows, shifts):
    n = lax.axis_size("span")
    nz, nx = first_exposure.shape[1:]
    x_blocks = (PAD_X + nx + PAD_X) // SUB
    hbm = pl.BlockSpec(memory_space=pltpu.HBM)
    return pl.pallas_call(
        functools.partial(kernel, n),
        name="update",
        out_shape=jax.ShapeDtypeStruct((3, CY // STRIDE, GZX), F32),
        in_specs=[hbm] * 4,
        out_specs=pl.BlockSpec(memory_space=pltpu.VMEM),
        scratch_shapes=[
            pltpu.SMEM(windows.shape, jnp.int32),
            pltpu.SMEM(shifts.shape, jnp.int32),
            pltpu.VMEM((CY, nz, nx), BF16),
            pltpu.VMEM((CY, nz, nx), BF16),
            pltpu.VMEM((HALO, nz, nx), BF16),
            pltpu.VMEM((HALO, nz, nx), BF16),
            pltpu.SMEM(windows.shape, jnp.int32),
            pltpu.SMEM(windows.shape, jnp.int32),
            pltpu.SMEM(shifts.shape, jnp.int32),
            pltpu.SMEM(shifts.shape, jnp.int32),
            pltpu.VMEM((A_PLANES * x_blocks, SUB, LANES), BF16),
            pltpu.VMEM((3 * B_PLANES * x_blocks + 1, SUB, LANES), BF16),
            *(pltpu.VMEM((p + 4, XR, LANES), BF16) for p in PLANES),
            pltpu.VMEM((TASKS, SUB, LANES), BF16),
            pltpu.VMEM((2, CY // STEP + 1, nx // SUB, SUB, LANES), F32),
            pltpu.VMEM((2, CY + 2 * HALO + 1, nx // SUB, SUB, LANES), F32),
            pltpu.VMEM((LINES, TASKS, 3 * XR), F32),
            pltpu.VMEM((8, 4 * LANES), F32),
            pltpu.VMEM((8, 4 * LANES), F32),
            pltpu.VMEM((8, 4 * LANES), F32),
            pltpu.SemaphoreType.DMA((8,)),
            pltpu.SemaphoreType.DMA((8,)),
            pltpu.SemaphoreType.DMA((2 * (CY // PREP) + 2,)),
        ],
        compiler_params=pltpu.CompilerParams(
            collective_id=0, has_side_effects=True, vmem_limit_bytes=VMEM_BYTES
        ),
    )(windows, shifts, first_exposure, second_exposure)


def solution(mesh):
    in_specs = (
        P(("grp", "span"), None, None),
        P(("grp", "span"), None, None),
        P(("grp", "span")),
        P(None, ("grp", "span")),
    )
    out_specs = P(None, ("grp", "span"), None)
    return jax.shard_map(shards, mesh=mesh, in_specs=in_specs, out_specs=out_specs, check_vma=False)
```
